1024 devices in a mesh: sens: 4 (over y_hi), par: 256 (over z, x, y_lo, core).
Axes of the slice: x: 4, y: 8 (y_hi: 4, y_lo: 2; y = y_hi * 2 + y_lo), z: 16, core: 2. Of those that a mesh axis runs over, the one named last changes fastest.
Arguments:
- probes: bfloat16 [2, 512, 8192], P(None, 'sens', 'par'), may hold values from -6 to 6
- green_blocks: bfloat16 [2, 262144, 512], P(None, 'par', 'sens'), may hold values from -0.25 to 0.25
- noise_table: float32 [64, 8], replicated, may hold values from 0.3 to 4
- station_class: int32 [512], P('sens'), may hold values from 0 to 7
- kappa_table: float32 [16], replicated, may hold values from 0.1 to 4
- coeff_index: int32 [4096], replicated, may hold values from 0 to 15
Outputs:
- hess_probes: float32 [2, 512, 8192], P(None, 'sens', 'par')
The draws below stay inside these ranges and needn't reach their ends.
All inputs are finite; a program needn't handle non-finite values.
Results may differ from the reference program's by a relative error of at most 0.003.
Values may be sent and summed in bfloat16 or wider, within the bound.
A program may use at most 32 MiB of HBM per device.

```python
import math
import jax
import jax.numpy as jnp
from jax import lax

SPLIT = 4
DIP = 32
PROBES = 128
CLASSES = 16
GROUPS = 8
NFREQ = 64
SENSORS = 512
STRIKE = 128
CELLS = 4096
ROWS = 8192


def set_ends(entries, own_key, smallest, largest):
    dims = entries.shape
    index_at = [jax.random.randint(jax.random.fold_in(own_key, axis), (), 0, dims[axis]) for axis in range(len(dims))]
    entries = entries.at[tuple(index_at)].set(smallest)
    longest = dims.index(max(dims))
    index_at[longest] = (index_at[longest] + 1) % dims[longest]
    return entries.at[tuple(index_at)].set(largest)


def block_levels(key, extent, shards, least, largest):
    def one(axis_at, parts):
        draws = jax.random.uniform(jax.random.fold_in(jax.random.fold_in(key, 6), axis_at), (parts,), jnp.float32, least / len(shards), largest / len(shards))
        return jnp.repeat(jnp.exp(draws), extent[axis_at] // parts).reshape((-1,) + (1,) * (len(extent) - axis_at - 1))

    loudness = one(*shards[0])
    for cut in shards[1:]:
        loudness = loudness * one(*cut)
    return loudness


def normal_values(stream_key, dims, deviation, limit, shards=(), kind=jnp.bfloat16):
    loudness = block_levels(stream_key, dims, shards, -0.22, 0.18) if shards else 1.0
    result = jax.random.normal(stream_key, dims, jnp.float32) * deviation * loudness
    return jnp.minimum(jnp.maximum(result, -limit), limit).astype(kind)


def setup_inputs(seed: int = 0) -> dict:
    streams_of = jax.random.split(jax.random.key(seed), 7)
    return {
        "probes": normal_values(streams_of[0], (2, SENSORS, ROWS), 1.0, 6.0, ((1, 4), (2, 256))),
        "green_blocks": normal_values(streams_of[1], (2, NFREQ * CELLS, SENSORS), SENSORS ** -0.5, 0.25, ((1, 256), (2, 4))),
        "noise_table": jnp.clip(jnp.exp(jax.random.uniform(streams_of[2], (NFREQ, GROUPS), jnp.float32, math.log(0.3), math.log(4.0))), 0.3, 4.0),
        "station_class": set_ends(jax.random.randint(streams_of[3], (SENSORS,), 0, GROUPS), jax.random.fold_in(streams_of[3], 1), 0, GROUPS - 1).astype(jnp.int32),
        "kappa_table": jnp.clip(jnp.exp(jax.random.uniform(streams_of[4], (CLASSES,), jnp.float32, math.log(0.1), math.log(4.0))), 0.1, 4.0),
        "coeff_index": set_ends(jax.random.randint(streams_of[5], (CELLS,), 0, CLASSES), jax.random.fold_in(streams_of[5], 1), 0, CLASSES - 1).astype(jnp.int32),
    }


def neighbours(values):
    padded = jnp.pad(values, ((0, 0), (1, 1), (1, 1), (0, 0)))
    summed = padded[:, 2:, 1:-1] + padded[:, :-2, 1:-1]
    return summed + padded[:, 1:-1, 2:] + padded[:, 1:-1, :-2]

def reference(probes, green_blocks, noise_table, station_class, kappa_table, coeff_index):
    part_probes = PROBES // SPLIT
    part_cells = CELLS // SPLIT
    weight = 1.0 / jnp.sqrt(noise_table[:, station_class].T)
    wrow = jnp.tile(jnp.repeat(weight, part_probes, axis=1), (1, SPLIT))
    weighted = (wrow[None] * probes.astype(jnp.float32)).astype(jnp.bfloat16)
    weighted = weighted.reshape(2, SENSORS, SPLIT, NFREQ, part_probes)
    green_split = green_blocks.reshape(2, SPLIT, NFREQ, part_cells, SENSORS)
    diagonal = (4.0 + kappa_table[coeff_index]).reshape(1, STRIKE, DIP, 1)

    def one_freq(freq_pos):
        green_part = lax.dynamic_index_in_dim(green_split, freq_pos, 2, keepdims=False).reshape(2, CELLS, SENSORS)
        probe_part = lax.dynamic_index_in_dim(weighted, freq_pos, 3, keepdims=False).reshape(2, SENSORS, PROBES)
        real_src = jnp.dot(green_part[0], probe_part[0], preferred_element_type=jnp.float32) + jnp.dot(green_part[1], probe_part[1], preferred_element_type=jnp.float32)
        imag_src = jnp.dot(green_part[0], probe_part[1], preferred_element_type=jnp.float32) - jnp.dot(green_part[1], probe_part[0], preferred_element_type=jnp.float32)
        source = jnp.stack([real_src, imag_src]).reshape(2, STRIKE, DIP, PROBES)
        first_sweep = source / diagonal
        second_sweep = (source + neighbours(first_sweep)) / diagonal
        slip_tile = ((source + neighbours(second_sweep)) / diagonal).astype(jnp.bfloat16).reshape(2, CELLS, PROBES)
        real_data = jnp.dot(green_part[0].T, slip_tile[0], preferred_element_type=jnp.float32) - jnp.dot(green_part[1].T, slip_tile[1], preferred_element_type=jnp.float32)
        imag_data = jnp.dot(green_part[0].T, slip_tile[1], preferred_element_type=jnp.float32) + jnp.dot(green_part[1].T, slip_tile[0], preferred_element_type=jnp.float32)
        return jnp.stack([real_data, imag_data])
    data_sum = lax.map(one_freq, jnp.arange(NFREQ, dtype=jnp.int32))
    data_sum = data_sum.reshape(NFREQ, 2, SENSORS, SPLIT, part_probes)
    data_sum = data_sum.transpose(1, 2, 3, 0, 4).reshape(2, SENSORS, ROWS)
    return wrow[None] * data_sum
```

```python
import functools

import jax
import jax.numpy as jnp
from jax import lax
from jax.experimental import pallas as pl
from jax.experimental.pallas import tpu as pltpu
from jax.sharding import PartitionSpec as P

SPLIT = 4
SENS = 4
DIP = 32
MESH = pl.DeviceIdType.MESH
NT = (((1,), (1,)), ((), ()))


def kernel(
    nfreq, probes, noise, station, kappa, coeff, green, out,
    gbuf, zbuf, hsend, hrecv, ysend, yrecv, zsend, zrecv,
    own_sem, gs, gr, zys, zyr, zzs, zzr, hs, hr, ys, yr, zs, zr,
):
    sens = lax.axis_index("sens")
    par = lax.axis_index("par")
    part = par // nfreq
    freq = par % nfreq

    def sens_peer(k):
        return {"sens": (sens + k) % SENS, "par": par}

    def part_peer(j):
        return {"sens": sens, "par": (part + j) % SPLIT * nfreq + freq}

    def block_of(s):
        return s + part % 2 * (SENS - 1 - 2 * s)

    def send(src, dst, ssem, rsem, device):
        copy = pltpu.make_async_remote_copy(
            src_ref=src, dst_ref=dst, send_sem=ssem, recv_sem=rsem,
            device_id=device, device_id_type=MESH,
        )
        copy.start()
        return copy

    barrier = pltpu.get_barrier_semaphore()
    for k in range(1, SENS):
        pl.semaphore_signal(barrier, inc=1, device_id=sens_peer(k), device_id_type=MESH)
    for j in range(1, SPLIT):
        pl.semaphore_signal(barrier, inc=1, device_id=part_peer(j), device_id_type=MESH)

    cells = gbuf.shape[2]
    block = block_of(sens)
    own = pltpu.make_async_copy(
        green.at[:, pl.ds(pl.multiple_of(block * cells, cells), cells), :], gbuf.at[0], own_sem
    )
    own.start()

    lane = lax.broadcasted_iota(jnp.int32, noise.shape, 1)
    column = jnp.sum(jnp.where(lane == freq, noise[...], 0.0), axis=1, keepdims=True)
    group = lax.broadcasted_iota(jnp.int32, (noise.shape[0], station.shape[1]), 0)
    variance = jnp.sum(jnp.where(group == station[...], column, 0.0), axis=0, keepdims=True)
    weight = 1.0 / jnp.sqrt(variance)
    for c in range(2):
        zbuf[part, 0, c] = (weight * probes[c].astype(jnp.float32)).astype(jnp.bfloat16)

    pl.semaphore_wait(barrier, SENS - 1 + SPLIT - 1)

    zy = [
        send(zbuf.at[part, 0], zbuf.at[part, k], zys.at[k - 1], zyr.at[k - 1], sens_peer(k))
        for k in range(1, SENS)
    ]
    g = []
    for k in (1, 3, 2):
        theirs = block_of((sens + k) % SENS)
        rows = pl.ds(pl.multiple_of(theirs * cells, cells), cells)
        g.append(send(green.at[:, rows, :], gbuf.at[k], gs.at[k - 1], gr.at[k - 1], sens_peer(k)))

    place = part * SENS + block
    rows_all = coeff.shape[0]

    def inverse(row, keep):
        index = coeff[pl.ds((row + rows_all) % rows_all, 1), :]
        value = jnp.zeros(index.shape, jnp.float32)
        for n in range(kappa.shape[0]):
            value = jnp.where(index == n, kappa[n], value)
        value = jnp.where(keep, 1.0 / (4.0 + value), 0.0)
        return jnp.broadcast_to(value, (128, 128)).T

    first = place == 0
    last = place == SPLIT * SENS - 1
    before = inverse(2 * place - 1, jnp.logical_not(first))
    after = inverse(2 * place + 2, jnp.logical_not(last))
    inv = jnp.concatenate(
        [before[64:], inverse(2 * place, True), inverse(2 * place + 1, True), after[:64]], axis=0
    )
    inv = inv.reshape(12, DIP, 128)
    inv = jnp.concatenate([inv, inv], axis=2)

    for copy in zy:
        copy.wait()
    zz = [
        send(zbuf.at[part], zbuf.at[part], zzs.at[j - 1], zzr.at[j - 1], part_peer(j))
        for j in range(1, SPLIT)
    ]
    own.wait()
    for copy in zz:
        copy.wait()
    for copy in g:
        copy.wait()

    src = jnp.zeros((cells, 256), jnp.float32)
    for k in range(SENS):
        a = jnp.concatenate([gbuf[k, 0], gbuf[k, 1]], axis=1)
        z_re = zbuf[:, k, 0].reshape(128, 128)
        z_im = zbuf[:, k, 1].reshape(128, 128)
        b = jnp.concatenate(
            [jnp.concatenate([z_re, z_im], axis=1), jnp.concatenate([z_im, -z_re], axis=1)], axis=0
        )
        src += lax.dot_general(a, b, NT, preferred_element_type=jnp.float32)

    hsend[0] = src[:64].astype(jnp.bfloat16)
    hsend[1] = src[cells - 64 :].astype(jnp.bfloat16)

    def device_of(b):
        p = b // SENS
        r = b % SENS
        return {"sens": r + p % 2 * (SENS - 1 - 2 * r), "par": p * nfreq + freq}

    def rim(side, b):
        return pltpu.make_async_remote_copy(
            src_ref=hsend.at[side], dst_ref=hrecv.at[1 - side], send_sem=hs.at[side],
            recv_sem=hr.at[1 - side], device_id=device_of(b), device_id_type=MESH,
        )

    total = SPLIT * SENS

    @pl.when(place > 0)
    def _():
        rim(0, (place + total - 1) % total).start()

    @pl.when(place < total - 1)
    def _():
        rim(1, (place + 1) % total).start()

    @pl.when(place == 0)
    def _():
        hrecv[0] = jnp.zeros(hrecv.shape[1:], hrecv.dtype)

    @pl.when(place == total - 1)
    def _():
        hrecv[1] = jnp.zeros(hrecv.shape[1:], hrecv.dtype)

    @pl.when(place > 0)
    def _():
        copy = rim(0, (place + total - 1) % total)
        copy.wait_send()
        pltpu.make_async_remote_copy(
            src_ref=hsend.at[1], dst_ref=hrecv.at[0], send_sem=hs.at[1],
            recv_sem=hr.at[0], device_id=device_of((place + total - 1) % total), device_id_type=MESH,
        ).wait_recv()

    @pl.when(place < total - 1)
    def _():
        copy = rim(1, (place + 1) % total)
        copy.wait_send()
        pltpu.make_async_remote_copy(
            src_ref=hsend.at[0], dst_ref=hrecv.at[1], send_sem=hs.at[0],
            recv_sem=hr.at[1], device_id=device_of((place + 1) % total), device_id_type=MESH,
        ).wait_recv()

    full = jnp.concatenate(
        [hrecv[0].astype(jnp.float32), src, hrecv[1].astype(jnp.float32)], axis=0
    ).reshape(12, DIP, 256)

    def dips(u):
        zero = jnp.zeros((u.shape[0], 1, u.shape[2]), u.dtype)
        return jnp.concatenate([u[:, 1:], zero], axis=1) + jnp.concatenate([zero, u[:, :-1]], axis=1)

    u1 = full * inv
    u2 = (full[1:11] + u1[:10] + u1[2:] + dips(u1[1:11])) * inv[1:11]
    slip = (full[2:10] + u2[:8] + u2[2:] + dips(u2[1:9])) * inv[2:10]
    slip_t = slip.reshape(cells, 256).astype(jnp.bfloat16).T

    def data_of(k):
        b = jnp.concatenate([gbuf[k, 0], gbuf[k, 1]], axis=1)
        both = jnp.dot(slip_t, b, preferred_element_type=jnp.float32)
        return both[:128, :128] - both[128:, 128:], both[128:, :128] + both[:128, 128:]

    y = []
    for k in (2, 1, 3):
        re, im = data_of(k)
        ysend[k - 1, 0] = re
        ysend[k - 1, 1] = im
        y.append(
            send(ysend.at[k - 1], yrecv.at[k - 1], ys.at[k - 1], yr.at[k - 1], sens_peer(SENS - k))
        )
    re, im = data_of(0)
    for copy in y:
        copy.wait()
    total_data = []
    for c, part_sum in ((0, re), (1, im)):
        total_data.append(part_sum + yrecv[0, c] + yrecv[1, c] + yrecv[2, c])
    zc = []
    for p in range(SPLIT):
        for c in range(2):
            zsend[p, c] = total_data[c][p * 32 : (p + 1) * 32]
    for j in (2, 1, 3):
        zc.append(
            send(zsend.at[(part + SPLIT - j) % SPLIT], zrecv.at[j - 1], zs.at[j - 1], zr.at[j - 1], part_peer(SPLIT - j))
        )
    for copy in zc:
        copy.wait()
    for c in range(2):
        out[c] = weight * (zsend[part, c] + zrecv[0, c] + zrecv[1, c] + zrecv[2, c])


def shards(probes, green_blocks, noise_table, station_class, kappa_table, coeff_index):
    nfreq = noise_table.shape[0]
    bf16, f32 = jnp.bfloat16, jnp.float32
    dma = pltpu.SemaphoreType.DMA
    vmem = pl.BlockSpec(memory_space=pltpu.VMEM)
    result = pl.pallas_call(
        functools.partial(kernel, nfreq),
        out_shape=jax.ShapeDtypeStruct((2, 32, 128), f32),
        in_specs=[
            vmem, vmem, vmem, pl.BlockSpec(memory_space=pltpu.SMEM), vmem,
            pl.BlockSpec(memory_space=pl.ANY),
        ],
        out_specs=vmem,
        scratch_shapes=[
            pltpu.VMEM((4, 2, 256, 128), bf16),
            pltpu.VMEM((4, 4, 2, 32, 128), bf16),
            pltpu.VMEM((2, 64, 256), bf16),
            pltpu.VMEM((2, 64, 256), bf16),
            pltpu.VMEM((3, 2, 128, 128), f32),
            pltpu.VMEM((3, 2, 128, 128), f32),
            pltpu.VMEM((4, 2, 32, 128), f32),
            pltpu.VMEM((3, 2, 32, 128), f32),
            dma, dma((3,)), dma((3,)), dma((3,)), dma((3,)), dma((3,)), dma((3,)),
            dma((2,)), dma((2,)), dma((3,)), dma((3,)), dma((3,)), dma((3,)),
        ],
        compiler_params=pltpu.CompilerParams(collective_id=0, has_side_effects=True),
    )(
        probes.transpose(0, 2, 1), noise_table.T, station_class.reshape(1, -1), kappa_table,
        coeff_index.reshape(-1, 128), green_blocks,
    )
    return result.transpose(0, 2, 1)


def solution(mesh):
    in_specs = (P(None, "sens", "par"), P(None, "par", "sens"), P(), P("sens"), P(), P())
    out_specs = P(None, "sens", "par")
    return jax.shard_map(shards, mesh=mesh, in_specs=in_specs, out_specs=out_specs, check_vma=False)
```

```python
import functools

import jax
import jax.numpy as jnp
from jax import lax
from jax.experimental import pallas as pl
from jax.experimental.pallas import tpu as pltpu
from jax.sharding import PartitionSpec as P

SPLIT = 4
SENS = 4
DIP = 32
MESH = pl.DeviceIdType.MESH
NT = (((1,), (1,)), ((), ()))


def kernel(
    nfreq, probes, noise, station, kappa, coeff, green, out,
    gbuf, zbuf, hsend, hrecv, ysend, yrecv, tsum, zsend, zrecv,
    own_sem, gs, gr, zys, zyr, zzs, zzr, hs, hr, ys, yr, zs, zr,
):
    sens = lax.axis_index("sens")
    par = lax.axis_index("par")
    part = par // nfreq
    freq = par % nfreq

    def sens_peer(k):
        return {"sens": (sens + k) % SENS, "par": par}

    def part_peer(j):
        return {"sens": sens, "par": (part + j) % SPLIT * nfreq + freq}

    def block_of(s):
        return s + part % 2 * (SENS - 1 - 2 * s)

    def send(src, dst, ssem, rsem, device):
        copy = pltpu.make_async_remote_copy(
            src_ref=src, dst_ref=dst, send_sem=ssem, recv_sem=rsem,
            device_id=device, device_id_type=MESH,
        )
        copy.start()
        return copy

    barrier = pltpu.get_barrier_semaphore()
    for k in range(1, SENS):
        pl.semaphore_signal(barrier, inc=1, device_id=sens_peer(k), device_id_type=MESH)
    for j in range(1, SPLIT):
        pl.semaphore_signal(barrier, inc=1, device_id=part_peer(j), device_id_type=MESH)

    cells = gbuf.shape[2]
    block = block_of(sens)
    own = pltpu.make_async_copy(
        green.at[:, pl.ds(pl.multiple_of(block * cells, cells), cells), :], gbuf.at[0], own_sem
    )
    own.start()

    lane = lax.broadcasted_iota(jnp.int32, noise.shape, 1)
    column = jnp.sum(jnp.where(lane == freq, noise[...], 0.0), axis=1, keepdims=True)
    group = lax.broadcasted_iota(jnp.int32, (noise.shape[0], station.shape[1]), 0)
    variance = jnp.sum(jnp.where(group == station[...], column, 0.0), axis=0, keepdims=True)
    weight = 1.0 / jnp.sqrt(variance)
    for c in range(2):
        zbuf[part, 0, c] = (weight * probes[c].astype(jnp.float32)).astype(jnp.bfloat16)

    pl.semaphore_wait(barrier, SENS - 1 + SPLIT - 1)

    zy = [
        send(zbuf.at[part, 0], zbuf.at[part, k], zys.at[k - 1], zyr.at[k - 1], sens_peer(k))
        for k in range(1, SENS)
    ]
    g = []
    for k in (1, 3, 2):
        theirs = block_of((sens + k) % SENS)
        rows = pl.ds(pl.multiple_of(theirs * cells, cells), cells)
        g.append(send(green.at[:, rows, :], gbuf.at[k], gs.at[k - 1], gr.at[k - 1], sens_peer(k)))

    place = part * SENS + block
    rows_all = coeff.shape[0]

    def inverse(row, keep):
        index = coeff[pl.ds((row + rows_all) % rows_all, 1), :]
        value = jnp.zeros(index.shape, jnp.float32)
        for n in range(kappa.shape[0]):
            value = jnp.where(index == n, kappa[n], value)
        value = jnp.where(keep, 1.0 / (4.0 + value), 0.0)
        return jnp.broadcast_to(value, (128, 128)).T

    first = place == 0
    last = place == SPLIT * SENS - 1
    before = inverse(2 * place - 1, jnp.logical_not(first))
    after = inverse(2 * place + 2, jnp.logical_not(last))
    inv = jnp.concatenate(
        [before[64:], inverse(2 * place, True), inverse(2 * place + 1, True), after[:64]], axis=0
    )
    inv = inv.reshape(12, DIP, 128)
    inv = jnp.concatenate([inv, inv], axis=2)

    for copy in zy:
        copy.wait()
    zz = [
        send(zbuf.at[part], zbuf.at[part], zzs.at[j - 1], zzr.at[j - 1], part_peer(j))
        for j in range(1, SPLIT)
    ]
    own.wait()
    for copy in zz:
        copy.wait()
    for copy in g:
        copy.wait()

    src = jnp.zeros((cells, 256), jnp.float32)
    for k in range(SENS):
        a = jnp.concatenate([gbuf[k, 0], gbuf[k, 1]], axis=1)
        z_re = zbuf[:, k, 0].reshape(128, 128)
        z_im = zbuf[:, k, 1].reshape(128, 128)
        b = jnp.concatenate(
            [jnp.concatenate([z_re, z_im], axis=1), jnp.concatenate([z_im, -z_re], axis=1)], axis=0
        )
        src += lax.dot_general(a, b, NT, preferred_element_type=jnp.float32)

    hsend[0] = src[:64].astype(jnp.bfloat16)
    hsend[1] = src[cells - 64 :].astype(jnp.bfloat16)

    def device_of(b):
        p = b // SENS
        r = b % SENS
        return {"sens": r + p % 2 * (SENS - 1 - 2 * r), "par": p * nfreq + freq}

    def rim(side, b):
        return pltpu.make_async_remote_copy(
            src_ref=hsend.at[side], dst_ref=hrecv.at[1 - side], send_sem=hs.at[side],
            recv_sem=hr.at[1 - side], device_id=device_of(b), device_id_type=MESH,
        )

    total = SPLIT * SENS

    @pl.when(place > 0)
    def _():
        rim(0, (place + total - 1) % total).start()

    @pl.when(place < total - 1)
    def _():
        rim(1, (place + 1) % total).start()

    @pl.when(place == 0)
    def _():
        hrecv[0] = jnp.zeros(hrecv.shape[1:], hrecv.dtype)

    @pl.when(place == total - 1)
    def _():
        hrecv[1] = jnp.zeros(hrecv.shape[1:], hrecv.dtype)

    @pl.when(place > 0)
    def _():
        copy = rim(0, (place + total - 1) % total)
        copy.wait_send()
        pltpu.make_async_remote_copy(
            src_ref=hsend.at[1], dst_ref=hrecv.at[0], send_sem=hs.at[1],
            recv_sem=hr.at[0], device_id=device_of((place + total - 1) % total), device_id_type=MESH,
        ).wait_recv()

    @pl.when(place < total - 1)
    def _():
        copy = rim(1, (place + 1) % total)
        copy.wait_send()
        pltpu.make_async_remote_copy(
            src_ref=hsend.at[0], dst_ref=hrecv.at[1], send_sem=hs.at[0],
            recv_sem=hr.at[1], device_id=device_of((place + 1) % total), device_id_type=MESH,
        ).wait_recv()

    full = jnp.concatenate(
        [hrecv[0].astype(jnp.float32), src, hrecv[1].astype(jnp.float32)], axis=0
    ).reshape(12, DIP, 256)

    def dips(u):
        zero = jnp.zeros((u.shape[0], 1, u.shape[2]), u.dtype)
        return jnp.concatenate([u[:, 1:], zero], axis=1) + jnp.concatenate([zero, u[:, :-1]], axis=1)

    u1 = full * inv
    u2 = (full[1:11] + u1[:10] + u1[2:] + dips(u1[1:11])) * inv[1:11]
    slip = (full[2:10] + u2[:8] + u2[2:] + dips(u2[1:9])) * inv[2:10]
    slip_t = slip.reshape(cells, 256).astype(jnp.bfloat16).T

    def data_of(k):
        b = jnp.concatenate([gbuf[k, 0], gbuf[k, 1]], axis=1)
        both = jnp.dot(slip_t, b, preferred_element_type=jnp.float32)
        return both[:128, :128] - both[128:, 128:], both[128:, :128] + both[:128, 128:]

    y = []
    for k in (2, 1, 3):
        re, im = data_of(k)
        ysend[k - 1, 0] = re.astype(ysend.dtype)
        ysend[k - 1, 1] = im.astype(ysend.dtype)
        y.append(
            send(ysend.at[k - 1], yrecv.at[k - 1], ys.at[k - 1], yr.at[k - 1], sens_peer(SENS - k))
        )
    re, im = data_of(0)
    for copy in y:
        copy.wait()
    total_data = []
    for c, part_sum in ((0, re), (1, im)):
        total_data.append(part_sum + sum(yrecv[k, c].astype(jnp.float32) for k in range(SENS - 1)))
    zc = []
    for p in range(SPLIT):
        for c in range(2):
            tsum[p, c] = total_data[c][p * 32 : (p + 1) * 32]
            zsend[p, c] = total_data[c][p * 32 : (p + 1) * 32].astype(zsend.dtype)
    for j in (2, 1, 3):
        zc.append(
            send(zsend.at[(part + SPLIT - j) % SPLIT], zrecv.at[j - 1], zs.at[j - 1], zr.at[j - 1], part_peer(SPLIT - j))
        )
    for copy in zc:
        copy.wait()
    for c in range(2):
        out[c] = weight * (tsum[part, c] + sum(zrecv[j, c].astype(jnp.float32) for j in range(SPLIT - 1)))


def shards(probes, green_blocks, noise_table, station_class, kappa_table, coeff_index):
    nfreq = noise_table.shape[0]
    bf16, f32 = jnp.bfloat16, jnp.float32
    dma = pltpu.SemaphoreType.DMA
    vmem = pl.BlockSpec(memory_space=pltpu.VMEM)
    result = pl.pallas_call(
        functools.partial(kernel, nfreq),
        out_shape=pltpu.VMEM((2, 32, 128), f32),
        in_specs=[
            vmem, vmem, vmem, pl.BlockSpec(memory_space=pltpu.SMEM), vmem,
            pl.BlockSpec(memory_space=pl.ANY),
        ],
        out_specs=vmem,
        scratch_shapes=[
            pltpu.VMEM((4, 2, 256, 128), bf16),
            pltpu.VMEM((4, 4, 2, 32, 128), bf16),
            pltpu.VMEM((2, 64, 256), bf16),
            pltpu.VMEM((2, 64, 256), bf16),
            pltpu.VMEM((3, 2, 128, 128), bf16),
            pltpu.VMEM((3, 2, 128, 128), bf16),
            pltpu.VMEM((4, 2, 32, 128), f32),
            pltpu.VMEM((4, 2, 32, 128), bf16),
            pltpu.VMEM((3, 2, 32, 128), bf16),
            dma, dma((3,)), dma((3,)), dma((3,)), dma((3,)), dma((3,)), dma((3,)),
            dma((2,)), dma((2,)), dma((3,)), dma((3,)), dma((3,)), dma((3,)),
        ],
        compiler_params=pltpu.CompilerParams(collective_id=0, has_side_effects=True),
    )(
        probes.transpose(0, 2, 1), noise_table.T, station_class.reshape(1, -1), kappa_table,
        coeff_index.reshape(-1, 128), green_blocks,
    )
    return result.transpose(0, 2, 1)


def solution(mesh):
    in_specs = (P(None, "sens", "par"), P(None, "par", "sens"), P(), P("sens"), P(), P())
    out_specs = P(None, "sens", "par")
    return jax.shard_map(shards, mesh=mesh, in_specs=in_specs, out_specs=out_specs, check_vma=False)
```

```python
import functools

import jax
import jax.numpy as jnp
from jax import lax
from jax.experimental import pallas as pl
from jax.experimental.pallas import tpu as pltpu
from jax.sharding import PartitionSpec as P

SPLIT = 4
SENS = 4
DIP = 32
EDGE = 64
LANES = 128
MESH = pl.DeviceIdType.MESH
NT = (((1,), (1,)), ((), ()))
NEAR_FIRST = (1, 3, 2)


def kernel(
    nfreq, probes_hbm, noise_hbm, station_hbm, kappa_hbm, coeff_hbm, green, out,
    probes, noise, station, kappa, coeff, gbuf, zbuf, hsend, hrecv, ysend, yrecv, tsum, zsend, zrecv,
    in_sem, own_sem, answer, gs, gr, zys, zyr, cs, cr, hs, hr, ys, yr, zs, zr,
):
    sens = lax.axis_index("sens")
    par = lax.axis_index("par")
    part = par // nfreq
    freq = par % nfreq

    def sens_peer(k):
        return {"sens": (sens + k) % SENS, "par": par}

    def in_part(p):
        return {"sens": sens, "par": p * nfreq + freq}

    right, left = in_part((part + 1) % SPLIT), in_part((part + SPLIT - 1) % SPLIT)

    def block_of(s):
        return s + part % 2 * (SENS - 1 - 2 * s)

    def signal(sem, device):
        pl.semaphore_signal(sem, inc=1, device_id=device, device_id_type=MESH)

    def remote(src, dst, ssem, rsem, device):
        return pltpu.make_async_remote_copy(
            src_ref=src, dst_ref=dst, send_sem=ssem, recv_sem=rsem,
            device_id=device, device_id_type=MESH,
        )

    def send(*args):
        copy = remote(*args)
        copy.start()
        return copy

    barrier = pltpu.get_barrier_semaphore()
    for k in NEAR_FIRST:
        signal(barrier, sens_peer(k))

    @pl.when(part < SPLIT - 1)
    def _():
        signal(barrier, right)

    @pl.when(part == 0)
    def _():
        signal(barrier, left)

    inputs = [
        pltpu.make_async_copy(src, dst, in_sem.at[i])
        for i, (src, dst) in enumerate(
            ((noise_hbm, noise), (station_hbm, station), (probes_hbm, probes), (coeff_hbm, coeff), (kappa_hbm, kappa))
        )
    ]
    for copy in inputs:
        copy.start()
    cells = gbuf.shape[2]
    block = block_of(sens)
    own = pltpu.make_async_copy(
        green.at[:, pl.ds(pl.multiple_of(block * cells, cells), cells), :], gbuf.at[0], own_sem
    )
    own.start()
    for copy in inputs:
        copy.wait()

    lane = lax.broadcasted_iota(jnp.int32, noise.shape, 1)
    column = jnp.sum(jnp.where(lane == freq, noise[...], 0.0), axis=1, keepdims=True)
    group = lax.broadcasted_iota(jnp.int32, (noise.shape[0], station.shape[1]), 0)
    variance = jnp.sum(jnp.where(group == station[...], column, 0.0), axis=0, keepdims=True)
    weight = 1.0 / jnp.sqrt(variance)
    for c in range(2):
        zbuf[part, 0, c] = (weight * probes[c].astype(jnp.float32)).astype(jnp.bfloat16)

    pl.semaphore_wait(barrier, SENS - 1 + (part + 3) // 4 + part // 3)

    @pl.when(part > 0)
    def _():
        signal(answer.at[0], left)

    @pl.when(part == SPLIT - 1)
    def _():
        signal(answer.at[1], right)

    zy = {
        k: send(zbuf.at[part, 0], zbuf.at[part, k], zys.at[k - 1], zyr.at[k - 1], sens_peer(k))
        for k in NEAR_FIRST
    }
    g = {}
    spans = ((0, EDGE), (cells - EDGE, EDGE), (EDGE, cells - 2 * EDGE))
    for which in ((0, 1), (2,)):
        for k in NEAR_FIRST:
            theirs = block_of((sens + k) % SENS) * cells
            for e in which:
                first, count = spans[e]
                rows = pl.ds(pl.multiple_of(theirs + first, EDGE), count)
                g[k, e] = send(
                    green.at[:, rows, :], gbuf.at[k, :, pl.ds(first, count), :],
                    gs.at[k - 1, e], gr.at[k - 1, e], sens_peer(k),
                )

    place = part * SENS + block
    total = SPLIT * SENS
    rows_all = coeff.shape[0]

    def inverse(row, keep):
        index = coeff[pl.ds((row + rows_all) % rows_all, 1), :]
        value = jnp.zeros(index.shape, jnp.float32)
        for n in range(kappa.shape[0]):
            value = jnp.where(index == n, kappa[n], value)
        value = jnp.where(keep, 1.0 / (4.0 + value), 0.0)
        return jnp.broadcast_to(value, (LANES, LANES)).T

    before = inverse(2 * place - 1, place > 0)
    after = inverse(2 * place + 2, place < total - 1)
    inv = jnp.concatenate(
        [before[EDGE:], inverse(2 * place, True), inverse(2 * place + 1, True), after[:EDGE]], axis=0
    ).reshape(12, DIP, LANES)

    @pl.when(place == 0)
    def _():
        for h in range(2):
            hrecv[h, 0] = jnp.zeros(hrecv.shape[2:], hrecv.dtype)

    @pl.when(place == total - 1)
    def _():
        for h in range(2):
            hrecv[h, 1] = jnp.zeros(hrecv.shape[2:], hrecv.dtype)

    def probe_copy(way, c, k):
        spot = zbuf.at[c, k]
        return remote(spot, spot, cs.at[way, c, k], cr.at[c, k], (right, left)[way])

    order = (0, *NEAR_FIRST)

    def pass_on(way, c):
        for k in order:
            probe_copy(way, c, k).start()

    def arrived(c):
        for k in order:
            probe_copy(0, c, k).wait_recv()

    def relay(way, c):
        for k in order:
            probe_copy(0, c, k).wait_recv()
            probe_copy(way, c, k).start()

    def pass_own(ways, c):
        for k in order:
            if k > 0:
                zy[k].wait_recv()
            for way in ways:
                probe_copy(way, c, k).start()

    @pl.when(part == 0)
    def _():
        pl.semaphore_wait(answer.at[0], 1)
        pass_own((0,), 0)
        arrived(1)
        pl.semaphore_wait(answer.at[1], 1)
        pass_on(1, 0)
        pass_on(1, 1)

    @pl.when(part == 1)
    def _():
        pass_own((1,), 1)
        arrived(0)
        pl.semaphore_wait(answer.at[0], 1)
        pass_on(0, 1)
        pass_on(0, 0)

    @pl.when(part == 2)
    def _():
        pass_own((1,), 2)
        pl.semaphore_wait(answer.at[0], 1)
        pass_on(0, 2)
        arrived(1)
        arrived(0)

    @pl.when(part == 3)
    def _():
        pass_own((0, 1), 3)
        arrived(0)
        arrived(1)

    def probe_rows(h, k):
        z_re = zbuf[2 * h : 2 * h + 2, k, 0].reshape(EDGE, LANES)
        z_im = zbuf[2 * h : 2 * h + 2, k, 1].reshape(EDGE, LANES)
        return jnp.concatenate(
            [jnp.concatenate([z_re, z_im], axis=1), jnp.concatenate([z_im, -z_re], axis=1)], axis=0
        )

    def source(h, spans_of):
        result = 0.0
        for k in order:
            a = jnp.concatenate(
                [
                    jnp.concatenate([gbuf[k, c, pl.ds(first, count), :] for c in range(2)], axis=1)
                    for first, count in spans_of
                ],
                axis=0,
            )
            result += lax.dot_general(a, probe_rows(h, k), NT, preferred_element_type=jnp.float32)
        return result

    def device_of(b):
        p = b // SENS
        r = b % SENS
        return {"sens": r + p % 2 * (SENS - 1 - 2 * r), "par": p * nfreq + freq}

    def rim(h, side):
        other = device_of((place + (total - 1, 1)[side]) % total)
        return remote(hsend.at[h, side], hrecv.at[h, 1 - side], hs.at[h, side], hr.at[h, 1 - side], other)

    def edges(h):
        src = source(h, spans[:2])
        hsend[h, 0] = src[:EDGE].astype(jnp.bfloat16)
        hsend[h, 1] = src[EDGE:].astype(jnp.bfloat16)

        @pl.when(place > 0)
        def _():
            rim(h, 0).start()

        @pl.when(place < total - 1)
        def _():
            rim(h, 1).start()

        return src

    own.wait()
    for k in NEAR_FIRST:
        for e in (0, 1):
            g[k, e].wait_recv()
    edge = [edges(0)]

    @pl.when(part == 0)
    def _():
        relay(0, 3)
        arrived(2)

    @pl.when(part == 1)
    def _():
        relay(1, 2)
        arrived(3)

    @pl.when(part == 2)
    def _():
        arrived(3)

    @pl.when(part == 3)
    def _():
        arrived(2)

    edge.append(edges(1))
    for k in NEAR_FIRST:
        g[k, 2].wait_recv()
    middle = [source(h, spans[2:]) for h in range(2)]

    def dips(u):
        zero = jnp.zeros((u.shape[0], 1, u.shape[2]), u.dtype)
        return jnp.concatenate([u[:, 1:], zero], axis=1) + jnp.concatenate([zero, u[:, :-1]], axis=1)

    def sum_copy(c, k):
        return remote(
            ysend.at[k - 1, c], yrecv.at[k - 1, c], ys.at[c, k - 1], yr.at[c, k - 1], sens_peer(SENS - k)
        )

    for h in range(2):
        @pl.when(place > 0)
        def _():
            remote(hsend.at[h, 1], hrecv.at[h, 0], hs.at[h, 1], hr.at[h, 0], left).wait_recv()

        @pl.when(place < total - 1)
        def _():
            remote(hsend.at[h, 0], hrecv.at[h, 1], hs.at[h, 0], hr.at[h, 1], left).wait_recv()

        full = jnp.concatenate(
            [
                hrecv[h, 0].astype(jnp.float32), edge[h][:EDGE], middle[h], edge[h][EDGE:],
                hrecv[h, 1].astype(jnp.float32),
            ],
            axis=0,
        ).reshape(12, DIP, LANES)
        u1 = full * inv
        u2 = (full[1:11] + u1[:10] + u1[2:] + dips(u1[1:11])) * inv[1:11]
        slip = (full[2:10] + u2[:8] + u2[2:] + dips(u2[1:9])) * inv[2:10]
        slip_t = slip.reshape(cells, LANES).astype(jnp.bfloat16).T

        for k in (*NEAR_FIRST, 0):
            b = jnp.concatenate([gbuf[k, 0], gbuf[k, 1]], axis=1)
            both = jnp.dot(slip_t, b, preferred_element_type=jnp.float32)
            re = both[:EDGE, :LANES] - both[EDGE:, LANES:]
            im = both[EDGE:, :LANES] + both[:EDGE, LANES:]
            for c, value in ((0, re), (1, im)):
                for i in range(2):
                    piece = value[i * 32 : (i + 1) * 32]
                    if k == 0:
                        tsum[2 * h + i, c] = piece
                    else:
                        ysend[k - 1, 2 * h + i, c] = piece.astype(ysend.dtype)
        for i in range(2):
            for k in NEAR_FIRST:
                sum_copy(2 * h + i, k).start()

    def sens_sum(p, c):
        return tsum[p, c] + sum(yrecv[k, p, c].astype(jnp.float32) for k in range(SENS - 1))

    def share(c):
        slot = (part - c + SPLIT) % SPLIT - 1
        return remote(zsend.at[c], zrecv.at[slot], zs.at[c], zr.at[slot], in_part(c))

    for p in range(SPLIT):
        for k in NEAR_FIRST:
            sum_copy(p, k).wait_recv()

        @pl.when(part != p)
        def _():
            for c in range(2):
                zsend[p, c] = sens_sum(p, c).astype(zsend.dtype)
            share(p).start()

    mine = [sens_sum(part, c) for c in range(2)]
    for j in range(SPLIT - 1):
        remote(zsend.at[0], zrecv.at[j], zs.at[0], zr.at[j], left).wait_recv()
    for c in range(2):
        out[c] = weight * (mine[c] + sum(zrecv[j, c].astype(jnp.float32) for j in range(SPLIT - 1)))

    for copy in [*zy.values(), *g.values()]:
        copy.wait_send()

    def gone(way, c):
        for k in order:
            probe_copy(way, c, k).wait_send()

    for p, sent in enumerate((((0, 0), (1, 0), (1, 1), (0, 3)), ((1, 1), (0, 1), (0, 0), (1, 2)), ((1, 2), (0, 2)), ((0, 3), (1, 3)))):

        @pl.when(part == p)
        def _():
            for way, c in sent:
                gone(way, c)

    for h in range(2):

        @pl.when(place > 0)
        def _():
            rim(h, 0).wait_send()

        @pl.when(place < total - 1)
        def _():
            rim(h, 1).wait_send()

    for p in range(SPLIT):
        for k in NEAR_FIRST:
            sum_copy(p, k).wait_send()

        @pl.when(part != p)
        def _():
            share(p).wait_send()


def shards(probes, green_blocks, noise_table, station_class, kappa_table, coeff_index):
    nfreq = noise_table.shape[0]
    bf16, f32, i32 = jnp.bfloat16, jnp.float32, jnp.int32
    dma = pltpu.SemaphoreType.DMA
    coeff = coeff_index.reshape(-1, LANES)
    hbm = pl.BlockSpec(memory_space=pl.ANY)
    result = pl.pallas_call(
        functools.partial(kernel, nfreq),
        out_shape=pltpu.VMEM((2, 32, LANES), f32),
        in_specs=[hbm] * 6,
        out_specs=pl.BlockSpec(memory_space=pltpu.VMEM),
        scratch_shapes=[
            pltpu.VMEM((2, 32, LANES), bf16),
            pltpu.VMEM(noise_table.shape[::-1], f32),
            pltpu.VMEM((1, LANES), i32),
            pltpu.SMEM(kappa_table.shape, f32),
            pltpu.VMEM(coeff.shape, i32),
            pltpu.VMEM((4, 2, 256, LANES), bf16),
            pltpu.VMEM((4, 4, 2, 32, LANES), bf16),
            pltpu.VMEM((2, 2, EDGE, LANES), bf16),
            pltpu.VMEM((2, 2, EDGE, LANES), bf16),
            pltpu.VMEM((3, 4, 2, 32, LANES), bf16),
            pltpu.VMEM((3, 4, 2, 32, LANES), bf16),
            pltpu.VMEM((4, 2, 32, LANES), f32),
            pltpu.VMEM((4, 2, 32, LANES), bf16),
            pltpu.VMEM((3, 2, 32, LANES), bf16),
            dma((5,)), dma, pltpu.SemaphoreType.REGULAR((2,)),
            dma((3, 3)), dma((3, 3)), dma((3,)), dma((3,)), dma((2, 4, 4)), dma((4, 4)),
            dma((2, 2)), dma((2, 2)), dma((4, 3)), dma((4, 3)), dma((4,)), dma((3,)),
        ],
        compiler_params=pltpu.CompilerParams(collective_id=0, has_side_effects=True),
    )(
        probes.transpose(0, 2, 1), noise_table.T, station_class.reshape(1, -1), kappa_table,
        coeff, green_blocks,
    )
    return result.transpose(0, 2, 1)


def solution(mesh):
    in_specs = (P(None, "sens", "par"), P(None, "par", "sens"), P(), P("sens"), P(), P())
    out_specs = P(None, "sens", "par")
    return jax.shard_map(shards, mesh=mesh, in_specs=in_specs, out_specs=out_specs, check_vma=False)
```

```python
import functools

import jax
import jax.numpy as jnp
from jax import lax
from jax.experimental import pallas as pl
from jax.experimental.pallas import tpu as pltpu
from jax.sharding import PartitionSpec as P

SPLIT = 4
SENS = 4
DIP = 32
MESH = pl.DeviceIdType.MESH
NT = (((1,), (1,)), ((), ()))


def kernel(
    nfreq, probes_hbm, noise_hbm, station_hbm, kappa_hbm, coeff_hbm, green, out,
    probes, noise, station, kappa, coeff, in_sem, gbuf, zbuf, hsend, hrecv, ysend, yrecv, tsum, zsend, zrecv,
    own_sem, gs, gr, zys, zyr, rs, rr, ls, lr, fs, fr, hs, hr, ys, yr, zs, zr,
):
    sens = lax.axis_index("sens")
    par = lax.axis_index("par")
    part = par // nfreq
    freq = par % nfreq

    def sens_peer(k):
        return {"sens": (sens + k) % SENS, "par": par}

    def part_peer(j):
        return {"sens": sens, "par": (part + j) % SPLIT * nfreq + freq}

    def block_of(s):
        return s + part % 2 * (SENS - 1 - 2 * s)

    def send(src, dst, ssem, rsem, device):
        copy = pltpu.make_async_remote_copy(
            src_ref=src, dst_ref=dst, send_sem=ssem, recv_sem=rsem,
            device_id=device, device_id_type=MESH,
        )
        copy.start()
        return copy

    barrier = pltpu.get_barrier_semaphore()
    for k in range(1, SENS):
        pl.semaphore_signal(barrier, inc=1, device_id=sens_peer(k), device_id_type=MESH)
    for j in (1, SPLIT - 1):
        pl.semaphore_signal(barrier, inc=1, device_id=part_peer(j), device_id_type=MESH)

    inputs = [
        pltpu.make_async_copy(src, dst, in_sem.at[i])
        for i, (src, dst) in enumerate(
            ((noise_hbm, noise), (station_hbm, station), (probes_hbm, probes), (coeff_hbm, coeff), (kappa_hbm, kappa))
        )
    ]
    for copy in inputs:
        copy.start()
    cells = gbuf.shape[2]
    block = block_of(sens)
    own = pltpu.make_async_copy(
        green.at[:, pl.ds(pl.multiple_of(block * cells, cells), cells), :], gbuf.at[0], own_sem
    )
    own.start()

    for copy in inputs:
        copy.wait()

    lane = lax.broadcasted_iota(jnp.int32, noise.shape, 1)
    column = jnp.sum(jnp.where(lane == freq, noise[...], 0.0), axis=1, keepdims=True)
    group = lax.broadcasted_iota(jnp.int32, (noise.shape[0], station.shape[1]), 0)
    variance = jnp.sum(jnp.where(group == station[...], column, 0.0), axis=0, keepdims=True)
    weight = 1.0 / jnp.sqrt(variance)
    for c in range(2):
        zbuf[part, 0, c] = (weight * probes[c].astype(jnp.float32)).astype(jnp.bfloat16)

    pl.semaphore_wait(barrier, SENS - 1 + 2)

    right, left = (part + 1) % SPLIT, (part + 3) % SPLIT
    zy = {
        k: send(zbuf.at[part, 0], zbuf.at[part, k], zys.at[k - 1], zyr.at[k - 1], sens_peer(k))
        for k in (1, 3, 2)
    }

    def both_ways(k):
        block = zbuf.at[part, k]
        return (
            send(block, block, rs.at[k], rr.at[k], part_peer(1)),
            send(block, block, ls.at[k], lr.at[k], part_peer(3)),
        )

    ways = {0: both_ways(0)}
    core = par % 2

    def green_copy(k):
        theirs = block_of((sens + k) % SENS)
        rows = pl.ds(pl.multiple_of(theirs * cells, cells), cells)
        return pltpu.make_async_remote_copy(
            src_ref=green.at[:, rows, :], dst_ref=gbuf.at[k], send_sem=gs.at[k - 1], recv_sem=gr.at[k - 1],
            device_id=sens_peer(k), device_id_type=MESH,
        )

    g = {k: green_copy(k) for k in (1, 3, 2)}

    @pl.when(core == 0)
    def _():
        for k in (1, 3, 2):
            g[k].start()

    @pl.when(core == 1)
    def _():
        for k in ():
            g[k].start()

    place = part * SENS + block
    rows_all = coeff.shape[0]

    def inverse(row, keep):
        index = coeff[pl.ds((row + rows_all) % rows_all, 1), :]
        value = jnp.zeros(index.shape, jnp.float32)
        for n in range(kappa.shape[0]):
            value = jnp.where(index == n, kappa[n], value)
        value = jnp.where(keep, 1.0 / (4.0 + value), 0.0)
        return jnp.broadcast_to(value, (128, 128)).T

    first = place == 0
    last = place == SPLIT * SENS - 1
    before = inverse(2 * place - 1, jnp.logical_not(first))
    after = inverse(2 * place + 2, jnp.logical_not(last))
    inv = jnp.concatenate(
        [before[64:], inverse(2 * place, True), inverse(2 * place + 1, True), after[:64]], axis=0
    )
    inv = inv.reshape(12, DIP, 128)
    inv = jnp.concatenate([inv, inv], axis=2)

    for k in (1, 3, 2):
        zy[k].wait_recv()
        ways[k] = both_ways(k)
    @pl.when(core == 1)
    def _():
        for k in (1, 3, 2):
            g[k].start()

    passed = {}
    for k in (0, 1, 3, 2):
        to_right, to_left = ways[k]
        if k in (0, 3):
            to_right.wait_recv()
            block = zbuf.at[left, k]
            passed[k] = send(block, block, fs.at[k], fr.at[k], part_peer(1))
        else:
            to_left.wait_recv()
            block = zbuf.at[right, k]
            passed[k] = send(block, block, fs.at[k], fr.at[k], part_peer(3))

    def probe_rows(k):
        z_re = zbuf[:, k, 0].reshape(128, 128)
        z_im = zbuf[:, k, 1].reshape(128, 128)
        return jnp.concatenate(
            [jnp.concatenate([z_re, z_im], axis=1), jnp.concatenate([z_im, -z_re], axis=1)], axis=0
        )

    def source(k, *spans):
        a = jnp.concatenate(
            [
                jnp.concatenate([gbuf[k, c, pl.ds(first, count), :] for c in range(2)], axis=1)
                for first, count in spans
            ],
            axis=0,
        )
        return lax.dot_general(a, probe_rows(k), NT, preferred_element_type=jnp.float32)

    edge = 0.0
    for k in (0, 1, 3, 2):
        if k == 0:
            own.wait()
        else:
            g[k].wait_recv()
        ways[k][1 if k in (0, 3) else 0].wait_recv()
        passed[k].wait_recv()
        edge += source(k, (0, 64), (cells - 64, 64))

    hsend[0] = edge[:64].astype(jnp.bfloat16)
    hsend[1] = edge[64:].astype(jnp.bfloat16)

    def device_of(b):
        p = b // SENS
        r = b % SENS
        return {"sens": r + p % 2 * (SENS - 1 - 2 * r), "par": p * nfreq + freq}

    def rim(side, b):
        return pltpu.make_async_remote_copy(
            src_ref=hsend.at[side], dst_ref=hrecv.at[1 - side], send_sem=hs.at[side],
            recv_sem=hr.at[1 - side], device_id=device_of(b), device_id_type=MESH,
        )

    total = SPLIT * SENS

    @pl.when(place > 0)
    def _():
        rim(0, (place + total - 1) % total).start()

    @pl.when(place < total - 1)
    def _():
        rim(1, (place + 1) % total).start()

    middle = sum(source(k, (64, cells - 128)) for k in range(SENS))

    @pl.when(place == 0)
    def _():
        hrecv[0] = jnp.zeros(hrecv.shape[1:], hrecv.dtype)

    @pl.when(place == total - 1)
    def _():
        hrecv[1] = jnp.zeros(hrecv.shape[1:], hrecv.dtype)

    @pl.when(place > 0)
    def _():
        copy = rim(0, (place + total - 1) % total)
        copy.wait_send()
        pltpu.make_async_remote_copy(
            src_ref=hsend.at[1], dst_ref=hrecv.at[0], send_sem=hs.at[1],
            recv_sem=hr.at[0], device_id=device_of((place + total - 1) % total), device_id_type=MESH,
        ).wait_recv()

    @pl.when(place < total - 1)
    def _():
        copy = rim(1, (place + 1) % total)
        copy.wait_send()
        pltpu.make_async_remote_copy(
            src_ref=hsend.at[0], dst_ref=hrecv.at[1], send_sem=hs.at[0],
            recv_sem=hr.at[1], device_id=device_of((place + 1) % total), device_id_type=MESH,
        ).wait_recv()

    full = jnp.concatenate(
        [
            hrecv[0].astype(jnp.float32), edge[:64], middle, edge[64:],
            hrecv[1].astype(jnp.float32),
        ],
        axis=0,
    ).reshape(12, DIP, 256)

    def dips(u):
        zero = jnp.zeros((u.shape[0], 1, u.shape[2]), u.dtype)
        return jnp.concatenate([u[:, 1:], zero], axis=1) + jnp.concatenate([zero, u[:, :-1]], axis=1)

    u1 = full * inv
    u2 = (full[1:11] + u1[:10] + u1[2:] + dips(u1[1:11])) * inv[1:11]
    slip = (full[2:10] + u2[:8] + u2[2:] + dips(u2[1:9])) * inv[2:10]
    slip_t = slip.reshape(cells, 256).astype(jnp.bfloat16).T

    def data_of(k):
        b = jnp.concatenate([gbuf[k, 0], gbuf[k, 1]], axis=1)
        both = jnp.dot(slip_t, b, preferred_element_type=jnp.float32)
        return both[:128, :128] - both[128:, 128:], both[128:, :128] + both[:128, 128:]

    for k in range(SENS):
        for c, value in enumerate(data_of(k)):
            for p in range(SPLIT):
                piece = value[p * 32 : (p + 1) * 32]
                if k == 0:
                    tsum[p, c] = piece
                else:
                    ysend[k - 1, p, c] = piece.astype(ysend.dtype)

    y = {}
    for j in (2, 1, 3, 0):
        p = (part + j) % SPLIT
        for k in (2, 1, 3):
            y[j, k] = send(
                ysend.at[k - 1, p], yrecv.at[k - 1, p], ys.at[k - 1, j], yr.at[k - 1, j], sens_peer(SENS - k)
            )

    def sens_sum(j, c):
        p = (part + j) % SPLIT
        return tsum[p, c] + sum(yrecv[k, p, c].astype(jnp.float32) for k in range(SENS - 1))

    z = []
    for j in (2, 1, 3):
        for k in (1, 3, 2):
            y[j, k].wait_recv()
        for c in range(2):
            zsend[j - 1, c] = sens_sum(j, c).astype(zsend.dtype)
        z.append(send(zsend.at[j - 1], zrecv.at[j - 1], zs.at[j - 1], zr.at[j - 1], part_peer(j)))
    for k in (1, 3, 2):
        y[0, k].wait_recv()
    mine = [sens_sum(0, c) for c in range(2)]
    for copy in z:
        copy.wait_recv()
    for c in range(2):
        out[c] = weight * (mine[c] + sum(zrecv[j, c].astype(jnp.float32) for j in range(SPLIT - 1)))
    for copy in [*zy.values(), *g.values(), *passed.values(), *y.values(), *z]:
        copy.wait_send()
    for pair in ways.values():
        for copy in pair:
            copy.wait_send()


def shards(probes, green_blocks, noise_table, station_class, kappa_table, coeff_index):
    nfreq = noise_table.shape[0]
    bf16, f32 = jnp.bfloat16, jnp.float32
    dma = pltpu.SemaphoreType.DMA
    vmem = pl.BlockSpec(memory_space=pltpu.VMEM)
    result = pl.pallas_call(
        functools.partial(kernel, nfreq),
        out_shape=pltpu.VMEM((2, 32, 128), f32),
        in_specs=[pl.BlockSpec(memory_space=pl.ANY)] * 6,
        out_specs=vmem,
        scratch_shapes=[
            pltpu.VMEM((2, 32, 128), bf16),
            pltpu.VMEM(noise_table.shape[::-1], f32),
            pltpu.VMEM((1, 128), jnp.int32),
            pltpu.SMEM(kappa_table.shape, f32),
            pltpu.VMEM((32, 128), jnp.int32),
            dma((5,)),
            pltpu.VMEM((4, 2, 256, 128), bf16),
            pltpu.VMEM((4, 4, 2, 32, 128), bf16),
            pltpu.VMEM((2, 64, 256), bf16),
            pltpu.VMEM((2, 64, 256), bf16),
            pltpu.VMEM((3, 4, 2, 32, 128), bf16),
            pltpu.VMEM((3, 4, 2, 32, 128), bf16),
            pltpu.VMEM((4, 2, 32, 128), f32),
            pltpu.VMEM((3, 2, 32, 128), bf16),
            pltpu.VMEM((3, 2, 32, 128), bf16),
            dma, dma((3,)), dma((3,)), dma((3,)), dma((3,)),
            dma((4,)), dma((4,)), dma((4,)), dma((4,)), dma((4,)), dma((4,)),
            dma((2,)), dma((2,)), dma((3, 4)), dma((3, 4)), dma((3,)), dma((3,)),
        ],
        compiler_params=pltpu.CompilerParams(collective_id=0, has_side_effects=True),
    )(
        probes.transpose(0, 2, 1), noise_table.T, station_class.reshape(1, -1), kappa_table,
        coeff_index.reshape(-1, 128), green_blocks,
    )
    return result.transpose(0, 2, 1)


def solution(mesh):
    in_specs = (P(None, "sens", "par"), P(None, "par", "sens"), P(), P("sens"), P(), P())
    out_specs = P(None, "sens", "par")
    return jax.shard_map(shards, mesh=mesh, in_specs=in_specs, out_specs=out_specs, check_vma=False)
```

```python
import functools

import jax
import jax.numpy as jnp
from jax import lax
from jax.experimental import pallas as pl
from jax.experimental.pallas import tpu as pltpu
from jax.sharding import PartitionSpec as P

SPLIT = 4
SENS = 4
DIP = 32
MESH = pl.DeviceIdType.MESH
NT = (((1,), (1,)), ((), ()))


def kernel(
    nfreq, probes_hbm, noise_hbm, station_hbm, kappa_hbm, coeff_hbm, green, out,
    probes, noise, station, kappa, coeff, in_sem, gbuf, zbuf, hsend, hrecv, ysend, yrecv, tsum, zsend, zrecv,
    own_sem, gs, gr, zys, zyr, rs, rr, ls, lr, fs, fr, hs, hr, ys, yr, zs, zr,
):
    sens = lax.axis_index("sens")
    par = lax.axis_index("par")
    part = par // nfreq
    freq = par % nfreq

    def sens_peer(k):
        return {"sens": (sens + k) % SENS, "par": par}

    def part_peer(j):
        return {"sens": sens, "par": (part + j) % SPLIT * nfreq + freq}

    def block_of(s):
        return s + part % 2 * (SENS - 1 - 2 * s)

    def send(src, dst, ssem, rsem, device):
        copy = pltpu.make_async_remote_copy(
            src_ref=src, dst_ref=dst, send_sem=ssem, recv_sem=rsem,
            device_id=device, device_id_type=MESH,
        )
        copy.start()
        return copy

    barrier = pltpu.get_barrier_semaphore()
    for k in range(1, SENS):
        pl.semaphore_signal(barrier, inc=1, device_id=sens_peer(k), device_id_type=MESH)
    for j in (1, SPLIT - 1):
        pl.semaphore_signal(barrier, inc=1, device_id=part_peer(j), device_id_type=MESH)

    inputs = [
        pltpu.make_async_copy(src, dst, in_sem.at[i])
        for i, (src, dst) in enumerate(
            ((noise_hbm, noise), (station_hbm, station), (probes_hbm, probes), (coeff_hbm, coeff), (kappa_hbm, kappa))
        )
    ]
    for copy in inputs:
        copy.start()
    cells = gbuf.shape[2]
    block = block_of(sens)
    own = pltpu.make_async_copy(
        green.at[:, pl.ds(pl.multiple_of(block * cells, cells), cells), :], gbuf.at[0], own_sem
    )
    own.start()

    for copy in inputs:
        copy.wait()

    lane = lax.broadcasted_iota(jnp.int32, noise.shape, 1)
    column = jnp.sum(jnp.where(lane == freq, noise[...], 0.0), axis=1, keepdims=True)
    group = lax.broadcasted_iota(jnp.int32, (noise.shape[0], station.shape[1]), 0)
    variance = jnp.sum(jnp.where(group == station[...], column, 0.0), axis=0, keepdims=True)
    weight = 1.0 / jnp.sqrt(variance)
    for c in range(2):
        zbuf[part, 0, c] = (weight * probes[c].astype(jnp.float32)).astype(jnp.bfloat16)

    pl.semaphore_wait(barrier, SENS - 1 + 2)

    right, left = (part + 1) % SPLIT, (part + 3) % SPLIT
    zy = {
        k: send(zbuf.at[part, 0], zbuf.at[part, k], zys.at[k - 1], zyr.at[k - 1], sens_peer(k))
        for k in (1, 3, 2)
    }

    def both_ways(k):
        block = zbuf.at[part, k]
        return (
            send(block, block, rs.at[k], rr.at[k], part_peer(1)),
            send(block, block, ls.at[k], lr.at[k], part_peer(3)),
        )

    ways = {0: both_ways(0)}
    core = par % 2

    def green_copy(k):
        theirs = block_of((sens + k) % SENS)
        rows = pl.ds(pl.multiple_of(theirs * cells, cells), cells)
        return pltpu.make_async_remote_copy(
            src_ref=green.at[:, rows, :], dst_ref=gbuf.at[k], send_sem=gs.at[k - 1], recv_sem=gr.at[k - 1],
            device_id=sens_peer(k), device_id_type=MESH,
        )

    g = {k: green_copy(k) for k in (1, 3, 2)}

    @pl.when(core == 0)
    def _():
        for k in (1, 3, 2):
            g[k].start()

    @pl.when(core == 1)
    def _():
        for k in ():
            g[k].start()

    place = part * SENS + block
    rows_all = coeff.shape[0]

    def inverse(row, keep):
        index = coeff[pl.ds((row + rows_all) % rows_all, 1), :]
        value = jnp.zeros(index.shape, jnp.float32)
        for n in range(kappa.shape[0]):
            value = jnp.where(index == n, kappa[n], value)
        value = jnp.where(keep, 1.0 / (4.0 + value), 0.0)
        return jnp.broadcast_to(value, (128, 128)).T

    first = place == 0
    last = place == SPLIT * SENS - 1
    before = inverse(2 * place - 1, jnp.logical_not(first))
    after = inverse(2 * place + 2, jnp.logical_not(last))
    inv = jnp.concatenate(
        [before[64:], inverse(2 * place, True), inverse(2 * place + 1, True), after[:64]], axis=0
    )
    inv = inv.reshape(12, DIP, 128)
    inv = jnp.concatenate([inv, inv], axis=2)

    for k in (1, 3, 2):
        zy[k].wait_recv()
        ways[k] = both_ways(k)
    @pl.when(core == 1)
    def _():
        for k in (1, 3, 2):
            g[k].start()

    passed = {}
    for k in (0, 1, 3, 2):
        to_right, to_left = ways[k]
        if k in (0, 3):
            to_right.wait_recv()
            block = zbuf.at[left, k]
            passed[k] = send(block, block, fs.at[k], fr.at[k], part_peer(1))
        else:
            to_left.wait_recv()
            block = zbuf.at[right, k]
            passed[k] = send(block, block, fs.at[k], fr.at[k], part_peer(3))

    def probe_rows(k):
        z_re = zbuf[:, k, 0].reshape(128, 128)
        z_im = zbuf[:, k, 1].reshape(128, 128)
        return jnp.concatenate(
            [jnp.concatenate([z_re, z_im], axis=1), jnp.concatenate([z_im, -z_re], axis=1)], axis=0
        )

    def source(k, *spans):
        a = jnp.concatenate(
            [
                jnp.concatenate([gbuf[k, c, pl.ds(first, count), :] for c in range(2)], axis=1)
                for first, count in spans
            ],
            axis=0,
        )
        return lax.dot_general(a, probe_rows(k), NT, preferred_element_type=jnp.float32)

    edge = 0.0
    for k in (0, 1, 3, 2):
        if k == 0:
            own.wait()
        else:
            g[k].wait_recv()
        ways[k][1 if k in (0, 3) else 0].wait_recv()
        passed[k].wait_recv()
        edge += source(k, (0, 64), (cells - 64, 64))

    hsend[0] = edge[:64].astype(jnp.bfloat16)
    hsend[1] = edge[64:].astype(jnp.bfloat16)

    def device_of(b):
        p = b // SENS
        r = b % SENS
        return {"sens": r + p % 2 * (SENS - 1 - 2 * r), "par": p * nfreq + freq}

    def rim(side, b):
        return pltpu.make_async_remote_copy(
            src_ref=hsend.at[side], dst_ref=hrecv.at[1 - side], send_sem=hs.at[side],
            recv_sem=hr.at[1 - side], device_id=device_of(b), device_id_type=MESH,
        )

    total = SPLIT * SENS

    @pl.when(place > 0)
    def _():
        rim(0, (place + total - 1) % total).start()

    @pl.when(place < total - 1)
    def _():
        rim(1, (place + 1) % total).start()

    middle = sum(source(k, (64, cells - 128)) for k in range(SENS))

    def dips(u):
        zero = jnp.zeros((u.shape[0], 1, u.shape[2]), u.dtype)
        return jnp.concatenate([u[:, 1:], zero], axis=1) + jnp.concatenate([zero, u[:, :-1]], axis=1)

    own_src = jnp.concatenate([edge[:64], middle, edge[64:]], axis=0).reshape(8, DIP, 256)
    inv_o = inv[2:10]
    u1 = own_src * inv_o
    none = jnp.zeros((1, DIP, 256), jnp.float32)
    base2 = (
        own_src + jnp.concatenate([none, u1[:-1]], axis=0) + jnp.concatenate([u1[1:], none], axis=0) + dips(u1)
    )
    u2 = base2[1:7] * inv_o[1:7]
    slip = (own_src[2:6] + u2[:4] + u2[2:] + dips(u2[1:5])) * inv_o[2:6]
    inner_t = slip.reshape(128, 256).astype(jnp.bfloat16).T


    @pl.when(place == 0)
    def _():
        hrecv[0] = jnp.zeros(hrecv.shape[1:], hrecv.dtype)

    @pl.when(place == total - 1)
    def _():
        hrecv[1] = jnp.zeros(hrecv.shape[1:], hrecv.dtype)

    @pl.when(place > 0)
    def _():
        copy = rim(0, (place + total - 1) % total)
        copy.wait_send()
        pltpu.make_async_remote_copy(
            src_ref=hsend.at[1], dst_ref=hrecv.at[0], send_sem=hs.at[1],
            recv_sem=hr.at[0], device_id=device_of((place + total - 1) % total), device_id_type=MESH,
        ).wait_recv()

    @pl.when(place < total - 1)
    def _():
        copy = rim(1, (place + 1) % total)
        copy.wait_send()
        pltpu.make_async_remote_copy(
            src_ref=hsend.at[0], dst_ref=hrecv.at[1], send_sem=hs.at[0],
            recv_sem=hr.at[1], device_id=device_of((place + 1) % total), device_id_type=MESH,
        ).wait_recv()

    rim_l, rim_r = (hrecv[side].astype(jnp.float32).reshape(2, DIP, 256) for side in range(2))
    u1_l, u1_r = rim_l * inv[:2], rim_r * inv[10:]
    u2_0 = (base2[:1] + u1_l[1:]) * inv_o[:1]
    u2_7 = (base2[7:] + u1_r[:1]) * inv_o[7:]
    u2_l = (rim_l[1:] + u1_l[:1] + u1[:1] + dips(u1_l[1:])) * inv[1:2]
    u2_r = (rim_r[:1] + u1_r[1:] + u1[7:] + dips(u1_r[:1])) * inv[10:11]
    outer = jnp.concatenate(
        [
            (own_src[:1] + u2_l + u2[:1] + dips(u2_0)) * inv_o[:1],
            (own_src[1:2] + u2_0 + u2[1:2] + dips(u2[:1])) * inv_o[1:2],
            (own_src[6:7] + u2[4:5] + u2_7 + dips(u2[5:])) * inv_o[6:7],
            (own_src[7:] + u2[5:] + u2_r + dips(u2_7)) * inv_o[7:],
        ],
        axis=0,
    )
    slip_t = jnp.concatenate([inner_t, outer.reshape(128, 256).astype(jnp.bfloat16).T], axis=1)

    def data_of(k):
        b = jnp.concatenate(
            [
                jnp.concatenate([gbuf[k, c, pl.ds(first, count), :] for c in range(2)], axis=1)
                for first, count in ((64, cells - 128), (0, 64), (cells - 64, 64))
            ],
            axis=0,
        )
        both = jnp.dot(slip_t, b, preferred_element_type=jnp.float32)
        return both[:128, :128] - both[128:, 128:], both[128:, :128] + both[:128, 128:]

    for k in range(SENS):
        for c, value in enumerate(data_of(k)):
            for p in range(SPLIT):
                piece = value[p * 32 : (p + 1) * 32]
                if k == 0:
                    tsum[p, c] = piece
                else:
                    ysend[k - 1, p, c] = piece.astype(ysend.dtype)

    y = {}
    for j in (2, 1, 3, 0):
        p = (part + j) % SPLIT
        for k in (2, 1, 3):
            y[j, k] = send(
                ysend.at[k - 1, p], yrecv.at[k - 1, p], ys.at[k - 1, j], yr.at[k - 1, j], sens_peer(SENS - k)
            )

    def sens_sum(j, c):
        p = (part + j) % SPLIT
        return tsum[p, c] + sum(yrecv[k, p, c].astype(jnp.float32) for k in range(SENS - 1))

    z = []
    for j in (2, 1, 3):
        for k in (1, 3, 2):
            y[j, k].wait_recv()
        for c in range(2):
            zsend[j - 1, c] = sens_sum(j, c).astype(zsend.dtype)
        z.append(send(zsend.at[j - 1], zrecv.at[j - 1], zs.at[j - 1], zr.at[j - 1], part_peer(j)))
    for k in (1, 3, 2):
        y[0, k].wait_recv()
    mine = [sens_sum(0, c) for c in range(2)]
    for copy in z:
        copy.wait_recv()
    for c in range(2):
        out[c] = weight * (mine[c] + sum(zrecv[j, c].astype(jnp.float32) for j in range(SPLIT - 1)))
    for copy in [*zy.values(), *g.values(), *passed.values(), *y.values(), *z]:
        copy.wait_send()
    for pair in ways.values():
        for copy in pair:
            copy.wait_send()


def shards(probes, green_blocks, noise_table, station_class, kappa_table, coeff_index):
    nfreq = noise_table.shape[0]
    bf16, f32 = jnp.bfloat16, jnp.float32
    dma = pltpu.SemaphoreType.DMA
    vmem = pl.BlockSpec(memory_space=pltpu.VMEM)
    result = pl.pallas_call(
        functools.partial(kernel, nfreq),
        out_shape=pltpu.VMEM((2, 32, 128), f32),
        in_specs=[pl.BlockSpec(memory_space=pl.ANY)] * 6,
        out_specs=vmem,
        scratch_shapes=[
            pltpu.VMEM((2, 32, 128), bf16),
            pltpu.VMEM(noise_table.shape[::-1], f32),
            pltpu.VMEM((1, 128), jnp.int32),
            pltpu.SMEM(kappa_table.shape, f32),
            pltpu.VMEM((32, 128), jnp.int32),
            dma((5,)),
            pltpu.VMEM((4, 2, 256, 128), bf16),
            pltpu.VMEM((4, 4, 2, 32, 128), bf16),
            pltpu.VMEM((2, 64, 256), bf16),
            pltpu.VMEM((2, 64, 256), bf16),
            pltpu.VMEM((3, 4, 2, 32, 128), bf16),
            pltpu.VMEM((3, 4, 2, 32, 128), bf16),
            pltpu.VMEM((4, 2, 32, 128), f32),
            pltpu.VMEM((3, 2, 32, 128), bf16),
            pltpu.VMEM((3, 2, 32, 128), bf16),
            dma, dma((3,)), dma((3,)), dma((3,)), dma((3,)),
            dma((4,)), dma((4,)), dma((4,)), dma((4,)), dma((4,)), dma((4,)),
            dma((2,)), dma((2,)), dma((3, 4)), dma((3, 4)), dma((3,)), dma((3,)),
        ],
        compiler_params=pltpu.CompilerParams(collective_id=0, has_side_effects=True),
    )(
        probes.transpose(0, 2, 1), noise_table.T, station_class.reshape(1, -1), kappa_table,
        coeff_index.reshape(-1, 128), green_blocks,
    )
    return result.transpose(0, 2, 1)


def solution(mesh):
    in_specs = (P(None, "sens", "par"), P(None, "par", "sens"), P(), P("sens"), P(), P())
    out_specs = P(None, "sens", "par")
    return jax.shard_map(shards, mesh=mesh, in_specs=in_specs, out_specs=out_specs, check_vma=False)
```

```python
import functools

import jax
import jax.numpy as jnp
from jax import lax
from jax.experimental import pallas as pl
from jax.experimental.pallas import tpu as pltpu
from jax.sharding import PartitionSpec as P

SPLIT = 4
SENS = 4
DIP = 32
MESH = pl.DeviceIdType.MESH
NT = (((1,), (1,)), ((), ()))


def kernel(
    nfreq, probes_hbm, noise_hbm, station_hbm, kappa_hbm, coeff_hbm, green, out,
    probes, noise, station, kappa, coeff, in_sem, gbuf, zbuf, hsend, hrecv, ysend, yrecv, tsum, zsend, zrecv,
    own_sem, gs, gr, zys, zyr, rs, rr, ls, lr, fs, fr, hs, hr, ys, yr, zs, zr,
):
    sens = lax.axis_index("sens")
    par = lax.axis_index("par")
    part = par // nfreq
    freq = par % nfreq

    def sens_peer(k):
        return {"sens": (sens + k) % SENS, "par": par}

    def part_peer(j):
        return {"sens": sens, "par": (part + j) % SPLIT * nfreq + freq}

    def block_of(s):
        return s + part % 2 * (SENS - 1 - 2 * s)

    def send(src, dst, ssem, rsem, device):
        copy = pltpu.make_async_remote_copy(
            src_ref=src, dst_ref=dst, send_sem=ssem, recv_sem=rsem,
            device_id=device, device_id_type=MESH,
        )
        copy.start()
        return copy

    barrier = pltpu.get_barrier_semaphore()
    for k in range(1, SENS):
        pl.semaphore_signal(barrier, inc=1, device_id=sens_peer(k), device_id_type=MESH)
    for j in (1, SPLIT - 1):
        pl.semaphore_signal(barrier, inc=1, device_id=part_peer(j), device_id_type=MESH)

    inputs = [
        pltpu.make_async_copy(src, dst, in_sem.at[i])
        for i, (src, dst) in enumerate(
            ((noise_hbm, noise), (station_hbm, station), (probes_hbm, probes), (coeff_hbm, coeff), (kappa_hbm, kappa))
        )
    ]
    for copy in inputs:
        copy.start()
    cells = gbuf.shape[2]
    block = block_of(sens)
    own = pltpu.make_async_copy(
        green.at[:, pl.ds(pl.multiple_of(block * cells, cells), cells), :], gbuf.at[0], own_sem
    )
    own.start()

    for copy in inputs:
        copy.wait()

    lane = lax.broadcasted_iota(jnp.int32, noise.shape, 1)
    column = jnp.sum(jnp.where(lane == freq, noise[...], 0.0), axis=1, keepdims=True)
    group = lax.broadcasted_iota(jnp.int32, (noise.shape[0], station.shape[1]), 0)
    variance = jnp.sum(jnp.where(group == station[...], column, 0.0), axis=0, keepdims=True)
    weight = 1.0 / jnp.sqrt(variance)
    for c in range(2):
        zbuf[part, 0, c] = (weight * probes[c].astype(jnp.float32)).astype(jnp.bfloat16)

    pl.semaphore_wait(barrier, SENS - 1 + 2)

    right, left = (part + 1) % SPLIT, (part + 3) % SPLIT
    zy = {
        k: send(zbuf.at[part, 0], zbuf.at[part, k], zys.at[k - 1], zyr.at[k - 1], sens_peer(k))
        for k in (1, 3, 2)
    }

    def both_ways(k):
        block = zbuf.at[part, k]
        return (
            send(block, block, rs.at[k], rr.at[k], part_peer(1)),
            send(block, block, ls.at[k], lr.at[k], part_peer(3)),
        )

    ways = {0: both_ways(0)}
    core = par % 2

    def green_copy(k):
        theirs = block_of((sens + k) % SENS)
        rows = pl.ds(pl.multiple_of(theirs * cells, cells), cells)
        return pltpu.make_async_remote_copy(
            src_ref=green.at[:, rows, :], dst_ref=gbuf.at[k], send_sem=gs.at[k - 1], recv_sem=gr.at[k - 1],
            device_id=sens_peer(k), device_id_type=MESH,
        )

    g = {k: green_copy(k) for k in (1, 3, 2)}

    @pl.when(core == 0)
    def _():
        for k in (1, 3, 2):
            g[k].start()

    @pl.when(core == 1)
    def _():
        for k in ():
            g[k].start()

    place = part * SENS + block
    rows_all = coeff.shape[0]

    def inverse(row, keep):
        index = coeff[pl.ds((row + rows_all) % rows_all, 1), :]
        value = jnp.zeros(index.shape, jnp.float32)
        for n in range(kappa.shape[0]):
            value = jnp.where(index == n, kappa[n], value)
        value = jnp.where(keep, 1.0 / (4.0 + value), 0.0)
        return jnp.broadcast_to(value, (128, 128)).T

    first = place == 0
    last = place == SPLIT * SENS - 1
    before = inverse(2 * place - 1, jnp.logical_not(first))
    after = inverse(2 * place + 2, jnp.logical_not(last))
    inv = jnp.concatenate(
        [before[64:], inverse(2 * place, True), inverse(2 * place + 1, True), after[:64]], axis=0
    )
    inv = inv.reshape(12, DIP, 128)
    inv = jnp.concatenate([inv, inv], axis=2)

    for k in (1, 3, 2):
        zy[k].wait_recv()
        ways[k] = both_ways(k)
    @pl.when(core == 1)
    def _():
        for k in (2, 1, 3):
            g[k].start()

    passed = {}
    for k in (0, 1, 3, 2):
        to_right, to_left = ways[k]
        if k in (0, 3):
            to_right.wait_recv()
            block = zbuf.at[left, k]
            passed[k] = send(block, block, fs.at[k], fr.at[k], part_peer(1))
        else:
            to_left.wait_recv()
            block = zbuf.at[right, k]
            passed[k] = send(block, block, fs.at[k], fr.at[k], part_peer(3))

    def probe_rows(k):
        z_re = zbuf[:, k, 0].reshape(128, 128)
        z_im = zbuf[:, k, 1].reshape(128, 128)
        return jnp.concatenate(
            [jnp.concatenate([z_re, z_im], axis=1), jnp.concatenate([z_im, -z_re], axis=1)], axis=0
        )

    def source(k, *spans):
        a = jnp.concatenate(
            [
                jnp.concatenate([gbuf[k, c, pl.ds(first, count), :] for c in range(2)], axis=1)
                for first, count in spans
            ],
            axis=0,
        )
        return lax.dot_general(a, probe_rows(k), NT, preferred_element_type=jnp.float32)

    edge = 0.0
    for k in (0, 1, 3, 2):
        if k == 0:
            own.wait()
        else:
            g[k].wait_recv()
        ways[k][1 if k in (0, 3) else 0].wait_recv()
        passed[k].wait_recv()
        edge += source(k, (0, 64), (cells - 64, 64))

    hsend[0] = edge[:64].astype(jnp.bfloat16)
    hsend[1] = edge[64:].astype(jnp.bfloat16)

    def device_of(b):
        p = b // SENS
        r = b % SENS
        return {"sens": r + p % 2 * (SENS - 1 - 2 * r), "par": p * nfreq + freq}

    def rim(side, b):
        return pltpu.make_async_remote_copy(
            src_ref=hsend.at[side], dst_ref=hrecv.at[1 - side], send_sem=hs.at[side],
            recv_sem=hr.at[1 - side], device_id=device_of(b), device_id_type=MESH,
        )

    total = SPLIT * SENS

    @pl.when(place > 0)
    def _():
        rim(0, (place + total - 1) % total).start()

    @pl.when(place < total - 1)
    def _():
        rim(1, (place + 1) % total).start()

    middle = sum(source(k, (64, cells - 128)) for k in range(SENS))

    def dips(u):
        zero = jnp.zeros((u.shape[0], 1, u.shape[2]), u.dtype)
        return jnp.concatenate([u[:, 1:], zero], axis=1) + jnp.concatenate([zero, u[:, :-1]], axis=1)

    own_src = jnp.concatenate([edge[:64], middle, edge[64:]], axis=0).reshape(8, DIP, 256)
    inv_o = inv[2:10]
    u1 = own_src * inv_o
    none = jnp.zeros((1, DIP, 256), jnp.float32)
    base2 = (
        own_src + jnp.concatenate([none, u1[:-1]], axis=0) + jnp.concatenate([u1[1:], none], axis=0) + dips(u1)
    )
    u2 = base2[1:7] * inv_o[1:7]
    slip = (own_src[2:6] + u2[:4] + u2[2:] + dips(u2[1:5])) * inv_o[2:6]
    inner_t = slip.reshape(128, 256).astype(jnp.bfloat16).T


    @pl.when(place == 0)
    def _():
        hrecv[0] = jnp.zeros(hrecv.shape[1:], hrecv.dtype)

    @pl.when(place == total - 1)
    def _():
        hrecv[1] = jnp.zeros(hrecv.shape[1:], hrecv.dtype)

    @pl.when(place > 0)
    def _():
        copy = rim(0, (place + total - 1) % total)
        copy.wait_send()
        pltpu.make_async_remote_copy(
            src_ref=hsend.at[1], dst_ref=hrecv.at[0], send_sem=hs.at[1],
            recv_sem=hr.at[0], device_id=device_of((place + total - 1) % total), device_id_type=MESH,
        ).wait_recv()

    @pl.when(place < total - 1)
    def _():
        copy = rim(1, (place + 1) % total)
        copy.wait_send()
        pltpu.make_async_remote_copy(
            src_ref=hsend.at[0], dst_ref=hrecv.at[1], send_sem=hs.at[0],
            recv_sem=hr.at[1], device_id=device_of((place + 1) % total), device_id_type=MESH,
        ).wait_recv()

    rim_l, rim_r = (hrecv[side].astype(jnp.float32).reshape(2, DIP, 256) for side in range(2))
    u1_l, u1_r = rim_l * inv[:2], rim_r * inv[10:]
    u2_0 = (base2[:1] + u1_l[1:]) * inv_o[:1]
    u2_7 = (base2[7:] + u1_r[:1]) * inv_o[7:]
    u2_l = (rim_l[1:] + u1_l[:1] + u1[:1] + dips(u1_l[1:])) * inv[1:2]
    u2_r = (rim_r[:1] + u1_r[1:] + u1[7:] + dips(u1_r[:1])) * inv[10:11]
    outer = jnp.concatenate(
        [
            (own_src[:1] + u2_l + u2[:1] + dips(u2_0)) * inv_o[:1],
            (own_src[1:2] + u2_0 + u2[1:2] + dips(u2[:1])) * inv_o[1:2],
            (own_src[6:7] + u2[4:5] + u2_7 + dips(u2[5:])) * inv_o[6:7],
            (own_src[7:] + u2[5:] + u2_r + dips(u2_7)) * inv_o[7:],
        ],
        axis=0,
    )
    slip_t = jnp.concatenate([inner_t, outer.reshape(128, 256).astype(jnp.bfloat16).T], axis=1)

    def data_of(k):
        b = jnp.concatenate(
            [
                jnp.concatenate([gbuf[k, c, pl.ds(first, count), :] for c in range(2)], axis=1)
                for first, count in ((64, cells - 128), (0, 64), (cells - 64, 64))
            ],
            axis=0,
        )
        both = jnp.dot(slip_t, b, preferred_element_type=jnp.float32)
        return both[:128, :128] - both[128:, 128:], both[128:, :128] + both[:128, 128:]

    for k in range(SENS):
        for c, value in enumerate(data_of(k)):
            for p in range(SPLIT):
                piece = value[p * 32 : (p + 1) * 32]
                if k == 0:
                    tsum[p, c] = piece
                else:
                    ysend[k - 1, p, c] = piece.astype(ysend.dtype)

    y = {}
    for j in (2, 1, 3, 0):
        p = (part + j) % SPLIT
        for k in (2, 1, 3):
            y[j, k] = send(
                ysend.at[k - 1, p], yrecv.at[k - 1, p], ys.at[k - 1, j], yr.at[k - 1, j], sens_peer(SENS - k)
            )

    def sens_sum(j, c):
        p = (part + j) % SPLIT
        return tsum[p, c] + sum(yrecv[k, p, c].astype(jnp.float32) for k in range(SENS - 1))

    z = []
    for j in (2, 1, 3):
        for k in (1, 3, 2):
            y[j, k].wait_recv()
        for c in range(2):
            zsend[j - 1, c] = sens_sum(j, c).astype(zsend.dtype)
        z.append(send(zsend.at[j - 1], zrecv.at[j - 1], zs.at[j - 1], zr.at[j - 1], part_peer(j)))
    for k in (1, 3, 2):
        y[0, k].wait_recv()
    mine = [sens_sum(0, c) for c in range(2)]
    for copy in z:
        copy.wait_recv()
    for c in range(2):
        out[c] = weight * (mine[c] + sum(zrecv[j, c].astype(jnp.float32) for j in range(SPLIT - 1)))
    for copy in [*zy.values(), *g.values(), *passed.values(), *y.values(), *z]:
        copy.wait_send()
    for pair in ways.values():
        for copy in pair:
            copy.wait_send()


def shards(probes, green_blocks, noise_table, station_class, kappa_table, coeff_index):
    nfreq = noise_table.shape[0]
    bf16, f32 = jnp.bfloat16, jnp.float32
    dma = pltpu.SemaphoreType.DMA
    vmem = pl.BlockSpec(memory_space=pltpu.VMEM)
    result = pl.pallas_call(
        functools.partial(kernel, nfreq),
        out_shape=pltpu.VMEM((2, 32, 128), f32),
        in_specs=[pl.BlockSpec(memory_space=pl.ANY)] * 6,
        out_specs=vmem,
        scratch_shapes=[
            pltpu.VMEM((2, 32, 128), bf16),
            pltpu.VMEM(noise_table.shape[::-1], f32),
            pltpu.VMEM((1, 128), jnp.int32),
            pltpu.SMEM(kappa_table.shape, f32),
            pltpu.VMEM((32, 128), jnp.int32),
            dma((5,)),
            pltpu.VMEM((4, 2, 256, 128), bf16),
            pltpu.VMEM((4, 4, 2, 32, 128), bf16),
            pltpu.VMEM((2, 64, 256), bf16),
            pltpu.VMEM((2, 64, 256), bf16),
            pltpu.VMEM((3, 4, 2, 32, 128), bf16),
            pltpu.VMEM((3, 4, 2, 32, 128), bf16),
            pltpu.VMEM((4, 2, 32, 128), f32),
            pltpu.VMEM((3, 2, 32, 128), bf16),
            pltpu.VMEM((3, 2, 32, 128), bf16),
            dma, dma((3,)), dma((3,)), dma((3,)), dma((3,)),
            dma((4,)), dma((4,)), dma((4,)), dma((4,)), dma((4,)), dma((4,)),
            dma((2,)), dma((2,)), dma((3, 4)), dma((3, 4)), dma((3,)), dma((3,)),
        ],
        compiler_params=pltpu.CompilerParams(collective_id=0, has_side_effects=True),
    )(
        probes.transpose(0, 2, 1), noise_table.T, station_class.reshape(1, -1), kappa_table,
        coeff_index.reshape(-1, 128), green_blocks,
    )
    return result.transpose(0, 2, 1)


def solution(mesh):
    in_specs = (P(None, "sens", "par"), P(None, "par", "sens"), P(), P("sens"), P(), P())
    out_specs = P(None, "sens", "par")
    return jax.shard_map(shards, mesh=mesh, in_specs=in_specs, out_specs=out_specs, check_vma=False)
```

```python
import functools

import jax
import jax.numpy as jnp
from jax import lax
from jax.experimental import pallas as pl
from jax.experimental.pallas import tpu as pltpu
from jax.sharding import PartitionSpec as P

SPLIT = 4
SENS = 4
DIP = 32
MESH = pl.DeviceIdType.MESH
NT = (((1,), (1,)), ((), ()))


def kernel(
    nfreq, probes_hbm, noise_hbm, station_hbm, kappa_hbm, coeff_hbm, green, out,
    probes, noise, station, kappa, coeff, in_sem, gbuf, zbuf, hsend, hrecv, ysend, yrecv, tsum, zsend, zrecv,
    own_sem, gs, gr, zys, zyr, rs, rr, ls, lr, fs, fr, hs, hr, ys, yr, zs, zr,
):
    sens = lax.axis_index("sens")
    par = lax.axis_index("par")
    part = par // nfreq
    freq = par % nfreq

    def sens_peer(k):
        return {"sens": (sens + k) % SENS, "par": par}

    def part_peer(j):
        return {"sens": sens, "par": (part + j) % SPLIT * nfreq + freq}

    def block_of(s):
        return s + part % 2 * (SENS - 1 - 2 * s)

    def send(src, dst, ssem, rsem, device):
        copy = pltpu.make_async_remote_copy(
            src_ref=src, dst_ref=dst, send_sem=ssem, recv_sem=rsem,
            device_id=device, device_id_type=MESH,
        )
        copy.start()
        return copy

    barrier = pltpu.get_barrier_semaphore()
    for k in range(1, SENS):
        pl.semaphore_signal(barrier, inc=1, device_id=sens_peer(k), device_id_type=MESH)
    for j in (1, SPLIT - 1):
        pl.semaphore_signal(barrier, inc=1, device_id=part_peer(j), device_id_type=MESH)

    inputs = [
        pltpu.make_async_copy(src, dst, in_sem.at[i])
        for i, (src, dst) in enumerate(
            ((noise_hbm, noise), (station_hbm, station), (probes_hbm, probes), (coeff_hbm, coeff), (kappa_hbm, kappa))
        )
    ]
    for copy in inputs:
        copy.start()
    cells = gbuf.shape[2]
    block = block_of(sens)
    own = pltpu.make_async_copy(
        green.at[:, pl.ds(pl.multiple_of(block * cells, cells), cells), :], gbuf.at[0], own_sem
    )
    own.start()

    for copy in inputs:
        copy.wait()

    lane = lax.broadcasted_iota(jnp.int32, noise.shape, 1)
    column = jnp.sum(jnp.where(lane == freq, noise[...], 0.0), axis=1, keepdims=True)
    group = lax.broadcasted_iota(jnp.int32, (noise.shape[0], station.shape[1]), 0)
    variance = jnp.sum(jnp.where(group == station[...], column, 0.0), axis=0, keepdims=True)
    weight = 1.0 / jnp.sqrt(variance)
    for c in range(2):
        zbuf[part, 0, c] = (weight * probes[c].astype(jnp.float32)).astype(jnp.bfloat16)

    pl.semaphore_wait(barrier, SENS - 1 + 2)

    right, left = (part + 1) % SPLIT, (part + 3) % SPLIT
    zy = {
        k: send(zbuf.at[part, 0], zbuf.at[part, k], zys.at[k - 1], zyr.at[k - 1], sens_peer(k))
        for k in (2, 1, 3)
    }

    def both_ways(k):
        block = zbuf.at[part, k]
        return (
            send(block, block, rs.at[k], rr.at[k], part_peer(1)),
            send(block, block, ls.at[k], lr.at[k], part_peer(3)),
        )

    ways = {0: both_ways(0)}
    core = par % 2

    def green_copy(k):
        theirs = block_of((sens + k) % SENS)
        rows = pl.ds(pl.multiple_of(theirs * cells, cells), cells)
        return pltpu.make_async_remote_copy(
            src_ref=green.at[:, rows, :], dst_ref=gbuf.at[k], send_sem=gs.at[k - 1], recv_sem=gr.at[k - 1],
            device_id=sens_peer(k), device_id_type=MESH,
        )

    g = {k: green_copy(k) for k in (1, 3, 2)}

    @pl.when(core == 0)
    def _():
        for k in (1, 3, 2):
            g[k].start()

    @pl.when(core == 1)
    def _():
        for k in ():
            g[k].start()

    place = part * SENS + block
    rows_all = coeff.shape[0]

    def inverse(row, keep):
        index = coeff[pl.ds((row + rows_all) % rows_all, 1), :]
        value = jnp.zeros(index.shape, jnp.float32)
        for n in range(kappa.shape[0]):
            value = jnp.where(index == n, kappa[n], value)
        value = jnp.where(keep, 1.0 / (4.0 + value), 0.0)
        return jnp.broadcast_to(value, (128, 128)).T

    first = place == 0
    last = place == SPLIT * SENS - 1
    before = inverse(2 * place - 1, jnp.logical_not(first))
    after = inverse(2 * place + 2, jnp.logical_not(last))
    inv = jnp.concatenate(
        [before[64:], inverse(2 * place, True), inverse(2 * place + 1, True), after[:64]], axis=0
    )
    inv = inv.reshape(12, DIP, 128)
    inv = jnp.concatenate([inv, inv], axis=2)

    for k in (1, 3, 2):
        zy[k].wait_recv()
        ways[k] = both_ways(k)
    @pl.when(core == 1)
    def _():
        for k in (2, 1, 3):
            g[k].start()

    passed = {}
    for k in (0, 1, 3, 2):
        to_right, to_left = ways[k]
        if k in (0, 3):
            to_right.wait_recv()
            block = zbuf.at[left, k]
            passed[k] = send(block, block, fs.at[k], fr.at[k], part_peer(1))
        else:
            to_left.wait_recv()
            block = zbuf.at[right, k]
            passed[k] = send(block, block, fs.at[k], fr.at[k], part_peer(3))

    def probe_rows(k):
        z_re = zbuf[:, k, 0].reshape(128, 128)
        z_im = zbuf[:, k, 1].reshape(128, 128)
        return jnp.concatenate(
            [jnp.concatenate([z_re, z_im], axis=1), jnp.concatenate([z_im, -z_re], axis=1)], axis=0
        )

    def source(k, *spans):
        a = jnp.concatenate(
            [
                jnp.concatenate([gbuf[k, c, pl.ds(first, count), :] for c in range(2)], axis=1)
                for first, count in spans
            ],
            axis=0,
        )
        return lax.dot_general(a, probe_rows(k), NT, preferred_element_type=jnp.float32)

    edge = 0.0
    for k in (0, 1, 3, 2):
        if k == 0:
            own.wait()
        else:
            g[k].wait_recv()
        ways[k][1 if k in (0, 3) else 0].wait_recv()
        passed[k].wait_recv()
        edge += source(k, (0, 64), (cells - 64, 64))

    hsend[0] = edge[:64].astype(jnp.bfloat16)
    hsend[1] = edge[64:].astype(jnp.bfloat16)

    def device_of(b):
        p = b // SENS
        r = b % SENS
        return {"sens": r + p % 2 * (SENS - 1 - 2 * r), "par": p * nfreq + freq}

    def rim(side, b):
        return pltpu.make_async_remote_copy(
            src_ref=hsend.at[side], dst_ref=hrecv.at[1 - side], send_sem=hs.at[side],
            recv_sem=hr.at[1 - side], device_id=device_of(b), device_id_type=MESH,
        )

    total = SPLIT * SENS

    @pl.when(place > 0)
    def _():
        rim(0, (place + total - 1) % total).start()

    @pl.when(place < total - 1)
    def _():
        rim(1, (place + 1) % total).start()

    middle = sum(source(k, (64, cells - 128)) for k in range(SENS))

    def dips(u):
        zero = jnp.zeros((u.shape[0], 1, u.shape[2]), u.dtype)
        return jnp.concatenate([u[:, 1:], zero], axis=1) + jnp.concatenate([zero, u[:, :-1]], axis=1)

    own_src = jnp.concatenate([edge[:64], middle, edge[64:]], axis=0).reshape(8, DIP, 256)
    inv_o = inv[2:10]
    u1 = own_src * inv_o
    none = jnp.zeros((1, DIP, 256), jnp.float32)
    base2 = (
        own_src + jnp.concatenate([none, u1[:-1]], axis=0) + jnp.concatenate([u1[1:], none], axis=0) + dips(u1)
    )
    u2 = base2[1:7] * inv_o[1:7]
    slip = (own_src[2:6] + u2[:4] + u2[2:] + dips(u2[1:5])) * inv_o[2:6]
    inner_t = slip.reshape(128, 256).astype(jnp.bfloat16).T


    @pl.when(place == 0)
    def _():
        hrecv[0] = jnp.zeros(hrecv.shape[1:], hrecv.dtype)

    @pl.when(place == total - 1)
    def _():
        hrecv[1] = jnp.zeros(hrecv.shape[1:], hrecv.dtype)

    @pl.when(place > 0)
    def _():
        copy = rim(0, (place + total - 1) % total)
        copy.wait_send()
        pltpu.make_async_remote_copy(
            src_ref=hsend.at[1], dst_ref=hrecv.at[0], send_sem=hs.at[1],
            recv_sem=hr.at[0], device_id=device_of((place + total - 1) % total), device_id_type=MESH,
        ).wait_recv()

    @pl.when(place < total - 1)
    def _():
        copy = rim(1, (place + 1) % total)
        copy.wait_send()
        pltpu.make_async_remote_copy(
            src_ref=hsend.at[0], dst_ref=hrecv.at[1], send_sem=hs.at[0],
            recv_sem=hr.at[1], device_id=device_of((place + 1) % total), device_id_type=MESH,
        ).wait_recv()

    rim_l, rim_r = (hrecv[side].astype(jnp.float32).reshape(2, DIP, 256) for side in range(2))
    u1_l, u1_r = rim_l * inv[:2], rim_r * inv[10:]
    u2_0 = (base2[:1] + u1_l[1:]) * inv_o[:1]
    u2_7 = (base2[7:] + u1_r[:1]) * inv_o[7:]
    u2_l = (rim_l[1:] + u1_l[:1] + u1[:1] + dips(u1_l[1:])) * inv[1:2]
    u2_r = (rim_r[:1] + u1_r[1:] + u1[7:] + dips(u1_r[:1])) * inv[10:11]
    outer = jnp.concatenate(
        [
            (own_src[:1] + u2_l + u2[:1] + dips(u2_0)) * inv_o[:1],
            (own_src[1:2] + u2_0 + u2[1:2] + dips(u2[:1])) * inv_o[1:2],
            (own_src[6:7] + u2[4:5] + u2_7 + dips(u2[5:])) * inv_o[6:7],
            (own_src[7:] + u2[5:] + u2_r + dips(u2_7)) * inv_o[7:],
        ],
        axis=0,
    )
    slip_t = jnp.concatenate([inner_t, outer.reshape(128, 256).astype(jnp.bfloat16).T], axis=1)

    def data_of(k):
        b = jnp.concatenate(
            [
                jnp.concatenate([gbuf[k, c, pl.ds(first, count), :] for c in range(2)], axis=1)
                for first, count in ((64, cells - 128), (0, 64), (cells - 64, 64))
            ],
            axis=0,
        )
        both = jnp.dot(slip_t, b, preferred_element_type=jnp.float32)
        return both[:128, :128] - both[128:, 128:], both[128:, :128] + both[:128, 128:]

    for k in range(SENS):
        for c, value in enumerate(data_of(k)):
            for p in range(SPLIT):
                piece = value[p * 32 : (p + 1) * 32]
                if k == 0:
                    tsum[p, c] = piece
                else:
                    ysend[k - 1, p, c] = piece.astype(ysend.dtype)

    y = {}
    for j in (2, 1, 3, 0):
        p = (part + j) % SPLIT
        for k in (2, 1, 3):
            y[j, k] = send(
                ysend.at[k - 1, p], yrecv.at[k - 1, p], ys.at[k - 1, j], yr.at[k - 1, j], sens_peer(SENS - k)
            )

    def sens_sum(j, c):
        p = (part + j) % SPLIT
        return tsum[p, c] + sum(yrecv[k, p, c].astype(jnp.float32) for k in range(SENS - 1))

    z = []
    for j in (2, 1, 3):
        for k in (1, 3, 2):
            y[j, k].wait_recv()
        for c in range(2):
            zsend[j - 1, c] = sens_sum(j, c).astype(zsend.dtype)
        z.append(send(zsend.at[j - 1], zrecv.at[j - 1], zs.at[j - 1], zr.at[j - 1], part_peer(j)))
    for k in (1, 3, 2):
        y[0, k].wait_recv()
    mine = [sens_sum(0, c) for c in range(2)]
    for copy in z:
        copy.wait_recv()
    for c in range(2):
        out[c] = weight * (mine[c] + sum(zrecv[j, c].astype(jnp.float32) for j in range(SPLIT - 1)))
    for copy in [*zy.values(), *g.values(), *passed.values(), *y.values(), *z]:
        copy.wait_send()
    for pair in ways.values():
        for copy in pair:
            copy.wait_send()


def shards(probes, green_blocks, noise_table, station_class, kappa_table, coeff_index):
    nfreq = noise_table.shape[0]
    bf16, f32 = jnp.bfloat16, jnp.float32
    dma = pltpu.SemaphoreType.DMA
    vmem = pl.BlockSpec(memory_space=pltpu.VMEM)
    result = pl.pallas_call(
        functools.partial(kernel, nfreq),
        out_shape=pltpu.VMEM((2, 32, 128), f32),
        in_specs=[pl.BlockSpec(memory_space=pl.ANY)] * 6,
        out_specs=vmem,
        scratch_shapes=[
            pltpu.VMEM((2, 32, 128), bf16),
            pltpu.VMEM(noise_table.shape[::-1], f32),
            pltpu.VMEM((1, 128), jnp.int32),
            pltpu.SMEM(kappa_table.shape, f32),
            pltpu.VMEM((32, 128), jnp.int32),
            dma((5,)),
            pltpu.VMEM((4, 2, 256, 128), bf16),
            pltpu.VMEM((4, 4, 2, 32, 128), bf16),
            pltpu.VMEM((2, 64, 256), bf16),
            pltpu.VMEM((2, 64, 256), bf16),
            pltpu.VMEM((3, 4, 2, 32, 128), bf16),
            pltpu.VMEM((3, 4, 2, 32, 128), bf16),
            pltpu.VMEM((4, 2, 32, 128), f32),
            pltpu.VMEM((3, 2, 32, 128), bf16),
            pltpu.VMEM((3, 2, 32, 128), bf16),
            dma, dma((3,)), dma((3,)), dma((3,)), dma((3,)),
            dma((4,)), dma((4,)), dma((4,)), dma((4,)), dma((4,)), dma((4,)),
            dma((2,)), dma((2,)), dma((3, 4)), dma((3, 4)), dma((3,)), dma((3,)),
        ],
        compiler_params=pltpu.CompilerParams(collective_id=0, has_side_effects=True),
    )(
        probes.transpose(0, 2, 1), noise_table.T, station_class.reshape(1, -1), kappa_table,
        coeff_index.reshape(-1, 128), green_blocks,
    )
    return result.transpose(0, 2, 1)


def solution(mesh):
    in_specs = (P(None, "sens", "par"), P(None, "par", "sens"), P(), P("sens"), P(), P())
    out_specs = P(None, "sens", "par")
    return jax.shard_map(shards, mesh=mesh, in_specs=in_specs, out_specs=out_specs, check_vma=False)
```
